768 devices in a mesh: gx: 16 (over y_lo, x), gy: 48 (over y_hi, z, core).
Axes of the slice: x: 4, y: 8 (y_hi: 2, y_lo: 4; y = y_hi * 4 + y_lo), z: 12, core: 2. Of those that a mesh axis runs over, the one named last changes fastest.
Arguments:
- positions: bfloat16 [16, 48, 3, 128], P('gx', 'gy'), may hold values from -0.5 to 0.5
- features: bfloat16 [16, 48, 128, 128], P('gx', 'gy'), may hold values from -6 to 6
- senders: int32 [16, 48, 1, 8], P('gx', 'gy'), may hold values from 0 to 8, as said below
- counts: int32 [16, 48, 1], P('gx', 'gy'), may hold values from 1 to 5, as said below
- radial_w: float32 [2, 8, 128], replicated, may hold values from -0.36 to 0.36
- mix_w: bfloat16 [128, 128], replicated, may hold values from -0.5 to 0.5
- square_w: bfloat16 [128, 128], replicated, may hold values from -0.5 to 0.5
- cotangent: bfloat16 [16, 48, 128, 128], P('gx', 'gy'), may hold values from -6 to 6
Outputs:
- updated: bfloat16 [16, 48, 128, 128], P('gx', 'gy')
- grad_features: float32 [16, 48, 128, 128], P('gx', 'gy')
The draws below stay inside these ranges and needn't reach their ends.
Inputs may be any that keep to these rules, and one draw needn't show every extreme that they name: `senders`: an entry g names ghost block g of the receiver's cell (see the steps); the 8 entries of one receiver block differ. Over the 1 receiver blocks of one cell the counts sum to at most 5, and some cell reaches 5 in every draw.
All inputs are finite; a program needn't handle non-finite values.
Results may differ from the reference program's by a relative error of at most 0.005.
The reference program's roundings to bfloat16 on the way (of `stacked`, `basis`, `first_bf`, `second_bf`, `weighted` and `grad_basis`) count: a program that leaves them out, or rounds other values in their place, can miss the bound.
Values may be sent and summed in bfloat16 or wider, within the bound.
A program may use at most 32 MiB of HBM per device.

```python
import jax
import jax.numpy as jnp
from jax import lax

C = 128
NR = 8
BLK = 128
NB = 1
MAXT = 8
ATOMS = 128
LIVE = 5
N_GX = 16
N_GY = 48


def draw_senders(key, part):
    key_list = jax.random.split(jax.random.fold_in(key, 11), N_GX * N_GY * NB)

    def one_list(row_key):
        return jax.random.permutation(row_key, 9 * NB)[:MAXT]
    chosen = jax.vmap(one_list)(key_list)
    return chosen.reshape(N_GX, N_GY, NB, MAXT).astype(jnp.int32)


def draw_counts(key, part):
    first_key, second_key, third_key = jax.random.split(jax.random.fold_in(key, 23), 3)
    budget_top = 4 * NB
    surplus = jax.random.randint(first_key, (N_GX, N_GY, NB), 0, MAXT)
    budget = jax.random.randint(second_key, (N_GX, N_GY), 0, budget_top + 1)
    picked = jax.random.randint(third_key, (), 0, N_GX * N_GY)
    forced = (jnp.arange(N_GX * N_GY) == picked).reshape(N_GX, N_GY)
    budget = jnp.where(forced, budget_top, budget)
    surplus = jnp.where(forced[:, :, None], MAXT - 1, surplus)
    running = jnp.cumsum(surplus, axis=-1)
    earlier = running - surplus
    granted = jnp.maximum(jnp.minimum(running, budget[:, :, None]) - earlier, 0)
    return (1 + granted).astype(jnp.int32)


def block_levels(rng, extent, shards, low, high):
    def one(axis_at, parts):
        steps = jax.random.uniform(jax.random.fold_in(jax.random.fold_in(rng, 6), axis_at), (parts,), jnp.float32, low / len(shards), high / len(shards))
        return jnp.repeat(jnp.exp(steps), extent[axis_at] // parts).reshape((-1,) + (1,) * (len(extent) - axis_at - 1))

    factor_of = one(*shards[0])
    for cut in shards[1:]:
        factor_of = factor_of * one(*cut)
    return factor_of


def normal_values(rng, extent, spread, limit, shards=(), kind=jnp.bfloat16):
    result = spread * jax.random.normal(rng, extent, jnp.float32)
    if shards:
        result = result * block_levels(rng, extent, shards, -0.22, 0.18)
    return jnp.clip(result, -limit, limit).astype(kind)


def setup_inputs(seed: int = 0) -> dict:
    splits = jax.random.split(jax.random.key(seed), 9)
    positions = jnp.clip(jax.random.uniform(splits[0], (N_GX, N_GY, 3, ATOMS), jnp.float32, -0.5, 0.5) * block_levels(splits[0], (N_GX, N_GY, 3, ATOMS), ((0, 16), (1, 48)), -0.4, 0.0), -0.5, 0.5).astype(jnp.bfloat16)
    features = normal_values(splits[1], (N_GX, N_GY, ATOMS, C), 1.0, 6.0, ((0, 16), (1, 48)))
    senders = draw_senders(jax.random.fold_in(splits[8], 71), 0)
    counts = draw_counts(jax.random.fold_in(splits[8], 71), 0)
    radial_w = normal_values(splits[4], (2, NR, C), 0.06, 0.36, (), jnp.float32)
    mix_w = normal_values(splits[5], (C, C), C ** -0.5, 0.5)
    square_w = normal_values(splits[6], (C, C), C ** -0.5, 0.5)
    cotangent = normal_values(splits[7], (N_GX, N_GY, ATOMS, C), 1.0, 6.0, ((0, 16), (1, 48)))
    return dict(positions=positions, features=features, senders=senders, counts=counts, radial_w=radial_w, mix_w=mix_w, square_w=square_w, cotangent=cotangent)


cutoff = 1.0
cell_side = 1.0

def tile_basis(recv_pos, send_pos, keep_mask, radial_count):
    displace = send_pos[:, None, :] - recv_pos[:, :, None]
    distance = jnp.sqrt(lax.optimization_barrier(jnp.sum(displace * displace, axis=0)))
    scaled = jnp.minimum(distance / cutoff, 1.0)
    envelope = (1.0 - scaled) * (1.0 - scaled) * keep_mask
    degrees = jnp.arange(radial_count).astype(jnp.float32)
    cosines = jnp.cos(jnp.pi * degrees[:, None, None] * scaled[None, :, :])
    return (cosines * envelope[None, :, :]).astype(jnp.bfloat16)

def place_ghosts(ghost_pos):
    shift_values = (jnp.arange(3) - 1).astype(jnp.float32) * cell_side
    component = jnp.arange(3)
    along_x = shift_values[:, None, None, None] * (component == 0).astype(jnp.float32)[None, None, :, None]
    along_y = shift_values[None, :, None, None] * (component == 1).astype(jnp.float32)[None, None, :, None]
    placed = ghost_pos.astype(jnp.float32) + along_x + along_y
    return placed.reshape(9, 3, ghost_pos.shape[3])

def tile_list(senders, counts, keep_count):
    block_count = senders.shape[0]
    slot_count = senders.shape[1]
    flat_slots = jnp.arange(block_count * slot_count, dtype=jnp.int32)
    receiver = flat_slots // slot_count
    slot_index = flat_slots % slot_count
    sender = senders.reshape(-1).astype(jnp.int32)
    active = slot_index < counts[receiver]
    if keep_count < block_count * slot_count:
        arranged = jnp.argsort(jnp.where(active, 0, 1).astype(jnp.int32), stable=True)[:keep_count]
        return (receiver[arranged], sender[arranged], active[arranged])
    return (receiver, sender, active)

def interact(own_pos, placed, ghost_feat, receiver, sender, active, grad_out, radial_w, mix_w, square_w):
    atom_count = own_pos.shape[1]
    channels = ghost_feat.shape[-1]
    radial_count = radial_w.shape[1]
    block_count = atom_count // BLK
    block_pos = placed.reshape(9, 3, block_count, BLK).transpose(0, 2, 1, 3).reshape(9 * block_count, 3, BLK)
    block_feat = ghost_feat.reshape(9 * block_count, BLK, channels).astype(jnp.float32)
    stacked = jnp.concatenate([block_feat] + [block_pos[:, component, :, None] * block_feat for component in range(3)], axis=-1).astype(jnp.bfloat16)
    recv_pos = own_pos.reshape(3, block_count, BLK).transpose(1, 0, 2)
    identity = jnp.eye(BLK, dtype=jnp.float32)
    radial_zero = radial_w[0]
    radial_one = radial_w[1]
    radial_three = jnp.tile(radial_one, (1, 3))

    def tile_mask(target, source, switch):
        own_block = (source == 4 * block_count + target).astype(jnp.float32)
        return switch.astype(jnp.float32) * (1.0 - own_block * identity)

    def forward_step(totals, item):
        target, source, switch = item
        basis = tile_basis(recv_pos[target], block_pos[source], tile_mask(target, source, switch), radial_count)
        operand = stacked[source]
        sum_zero = jnp.zeros((BLK, channels), jnp.float32)
        sum_one = jnp.zeros((BLK, channels), jnp.float32)
        moments = jnp.zeros((BLK, 3 * channels), jnp.float32)
        for degree in range(radial_count):
            product = jnp.dot(basis[degree], operand, preferred_element_type=jnp.float32)
            sum_zero = sum_zero + radial_zero[degree] * product[:, :channels]
            sum_one = sum_one + radial_one[degree] * product[:, :channels]
            moments = moments + radial_three[degree] * product[:, channels:]
        update = jnp.concatenate([sum_zero, sum_one, moments], axis=-1)
        totals = lax.dynamic_update_index_in_dim(totals, totals[target] + update, target, 0)
        return (totals, None)
    totals, _ = lax.scan(forward_step, jnp.zeros((block_count, BLK, 5 * channels), jnp.float32), (receiver, sender, active))
    totals = totals.reshape(atom_count, 5 * channels)
    atom_pos = own_pos.T
    sum_zero = totals[:, :channels]
    sum_one = totals[:, channels:2 * channels]
    moments = totals[:, 2 * channels:].reshape(atom_count, 3, channels)
    first_bf = sum_zero.astype(jnp.bfloat16)
    second_bf = ((moments - atom_pos[:, :, None] * sum_one[:, None, :]) / cutoff).astype(jnp.bfloat16)
    quadratic = jnp.dot(second_bf.reshape(atom_count * 3, channels), square_w, preferred_element_type=jnp.float32).reshape(atom_count, 3, channels)
    linear = jnp.dot(first_bf, mix_w, preferred_element_type=jnp.float32)
    updated = (linear + lax.optimization_barrier(jnp.sum(quadratic * second_bf.astype(jnp.float32), axis=1))).astype(jnp.bfloat16)
    cot_float = grad_out.astype(jnp.float32)
    contract_rows = (((1,), (1,)), ((), ()))
    grad_first = lax.dot_general(grad_out, mix_w, contract_rows, preferred_element_type=jnp.float32)
    weighted = (cot_float[:, None, :] * second_bf.astype(jnp.float32)).astype(jnp.bfloat16)
    grad_second = cot_float[:, None, :] * quadratic + lax.dot_general(weighted.reshape(atom_count * 3, channels), square_w, contract_rows, preferred_element_type=jnp.float32).reshape(atom_count, 3, channels)
    grad_moments = grad_second / cutoff
    grad_sum_one = -lax.optimization_barrier(jnp.sum(atom_pos[:, :, None] * grad_second, axis=1)) / cutoff
    grad_lead = radial_zero[:, None, :] * grad_first[None] + radial_one[:, None, :] * grad_sum_one[None]
    grad_rest = radial_three[:, None, :] * grad_moments.reshape(atom_count, 3 * channels)[None]
    grad_basis = jnp.concatenate([grad_lead, grad_rest], axis=-1).astype(jnp.bfloat16)
    grad_basis = grad_basis.reshape(radial_count, block_count, BLK, 4 * channels).transpose(1, 0, 2, 3)

    def backward_step(ghost_grad, item):
        target, source, switch = item
        basis = tile_basis(recv_pos[target], block_pos[source], tile_mask(target, source, switch), radial_count)
        pulled = lax.dot_general(basis, grad_basis[target], (((0, 1), (0, 1)), ((), ())), preferred_element_type=jnp.float32)
        source_pos = block_pos[source]
        contribution = pulled[:, :channels]
        for component in range(3):
            contribution = contribution + source_pos[component][:, None] * pulled[:, (component + 1) * channels:(component + 2) * channels]
        ghost_grad = lax.dynamic_update_index_in_dim(ghost_grad, ghost_grad[source] + contribution, source, 0)
        return (ghost_grad, None)
    ghost_grad, _ = lax.scan(backward_step, jnp.zeros((9 * block_count, BLK, channels), jnp.float32), (receiver, sender, active))
    return (updated, ghost_grad.reshape(9, atom_count, channels))

def reference(positions, features, senders, counts, radial_w, mix_w, square_w, cotangent):
    displacements = (-1, 0, 1)
    ghost_pos = jnp.stack([jnp.stack([jnp.roll(positions, (-step_x, -step_y), (0, 1)) for step_y in displacements], 2) for step_x in displacements], 2)
    ghost_feat = jnp.stack([jnp.stack([jnp.roll(features, (-step_x, -step_y), (0, 1)) for step_y in displacements], 2) for step_x in displacements], 2)

    def one_cell(own_pos, cell_ghost_pos, cell_ghost_feat, cell_senders, cell_counts, cell_cot):
        receiver, sender, active = tile_list(cell_senders, cell_counts, LIVE)
        return interact(own_pos.astype(jnp.float32), place_ghosts(cell_ghost_pos), cell_ghost_feat, receiver, sender, active, cell_cot, radial_w, mix_w, square_w)

    def one_row(items):
        return jax.vmap(one_cell)(*items)
    updated, ghost_grad = lax.map(one_row, (positions, ghost_pos, ghost_feat, senders, counts, cotangent))
    ghost_grad = ghost_grad.reshape(N_GX, N_GY, 3, 3, NB * BLK, C)
    gradient = jnp.zeros((N_GX, N_GY, NB * BLK, C), jnp.float32)
    for step_x in displacements:
        for step_y in displacements:
            gradient = gradient + jnp.roll(ghost_grad[:, :, step_x + 1, step_y + 1], (step_x, step_y), (0, 1))
    return (updated, gradient)
```

```python
import functools
import math

import jax
import jax.numpy as jnp
from jax import lax
from jax.experimental import pallas as pl
from jax.experimental.pallas import tpu as pltpu
from jax.sharding import PartitionSpec as P

MESH = pl.DeviceIdType.MESH
BLK = 128
CH = 128
NRAD = 8
GHOSTS = 9
OWN = 4
F32 = jnp.float32
BF16 = jnp.bfloat16

SERIES = [(-1.0) ** (n + 1) * math.pi ** (2 * n + 1) / math.factorial(2 * n + 1) for n in range(7)]


def radial(dx, dy, dz, keep):
    dist = jnp.sqrt(dx * dx + dy * dy + dz * dz)
    u = jnp.minimum(dist, 1.0)
    one_minus = 1.0 - u
    value = one_minus * one_minus * keep
    v = u - 0.5
    v2 = v * v
    acc = jnp.full_like(v2, SERIES[6])
    for coef in SERIES[5::-1]:
        acc = acc * v2 + coef
    cosine = acc * v
    twice = cosine + cosine
    out = [value, value * cosine]
    for _ in range(NRAD - 2):
        out.append(twice * out[-1] - out[-2])
    return [b.astype(BF16) for b in out]


def columns(rows):
    padded = jnp.concatenate([rows, jnp.zeros((BLK - 3, BLK), F32)], axis=0)
    return padded.T


def kernel(
    nx, ny,
    pos_ref, feat_ref, senders_ref, counts_ref, rad_ref, mix_ref, square_ref, cot_ref,
    updated_ref, grad_ref,
    gpos, gfeat, basis, basis_t, stack, gbasis, gcols, out_grad, in_grad,
    psend, precv, fsend, frecv, gsend, grecv,
):
    gx = lax.axis_index("gx")
    gy = lax.axis_index("gy")

    def peer(g):
        return (lax.rem(gx + (g // 3 - 1) + nx, nx), lax.rem(gy + (g % 3 - 1) + ny, ny))

    others = [g for g in range(GHOSTS) if g != OWN]
    barrier = pltpu.get_barrier_semaphore()
    for g in others:
        pl.semaphore_signal(barrier, inc=1, device_id=peer(g), device_id_type=MESH)
    pl.semaphore_wait(barrier, len(others))

    def pos_copy(g):
        return pltpu.make_async_remote_copy(
            src_ref=pos_ref.at[0, 0], dst_ref=gpos.at[8 - g], send_sem=psend.at[g],
            recv_sem=precv.at[8 - g], device_id=peer(g), device_id_type=MESH)

    def feat_copy(g):
        return pltpu.make_async_remote_copy(
            src_ref=feat_ref.at[0, 0], dst_ref=gfeat.at[8 - g], send_sem=fsend.at[g],
            recv_sem=frecv.at[8 - g], device_id=peer(g), device_id_type=MESH)

    def grad_copy(g):
        return pltpu.make_async_remote_copy(
            src_ref=out_grad.at[g], dst_ref=in_grad.at[8 - g], send_sem=gsend.at[g],
            recv_sem=grecv.at[8 - g], device_id=peer(g), device_id_type=MESH)

    for g in others:
        pos_copy(g).start()
    for g in others:
        feat_copy(g).start()

    own_rows = pos_ref[0, 0].astype(F32)
    own_cols = columns(own_rows)
    own_x = [own_rows[m:m + 1, :] for m in range(3)]
    own_c = [own_cols[:, m:m + 1] for m in range(3)]
    count = counts_ref[0, 0, 0]
    cot = cot_ref[0, 0]
    nt = (((1,), (1,)), ((), ()))
    grad_first = lax.dot_general(cot, mix_ref[...], nt, preferred_element_type=F32)
    diagonal = lax.broadcasted_iota(jnp.int32, (BLK, BLK), 0) == lax.broadcasted_iota(jnp.int32, (BLK, BLK), 1)

    def tile(p, own):
        g = lax.rem(p + OWN, GHOSTS)
        live = jnp.int32(0)
        for t in range(8):
            live = live + jnp.where((senders_ref[0, 0, 0, t] == g) & (t < count), 1, 0)
        keep = jnp.full((BLK, BLK), live.astype(F32))
        if own:
            keep = jnp.where(diagonal, 0.0, keep)
            rows = own_rows
        else:
            rows = gpos[g].astype(F32)
        shift = [(g // 3 - 1).astype(F32), (lax.rem(g, 3) - 1).astype(F32)]
        axis_of = lax.broadcasted_iota(jnp.int32, (3, BLK), 0)
        rows = rows + jnp.where(axis_of == 0, shift[0], jnp.where(axis_of == 1, shift[1], 0.0))
        cols = columns(rows)
        gcols[g] = cols
        line = [rows[m:m + 1, :] for m in range(3)]
        col = [cols[:, m:m + 1] for m in range(3)]
        lane = pl.ds(pl.multiple_of(g * BLK, BLK), BLK)
        for k, b in enumerate(radial(*[line[m] - own_c[m] for m in range(3)], keep)):
            basis[k * BLK:(k + 1) * BLK, lane] = b
        for k, b in enumerate(radial(*[col[m] - own_x[m] for m in range(3)], keep)):
            basis_t[lane, k * BLK:(k + 1) * BLK] = b

    def stack_tile(g, feat):
        cols = gcols[g]
        lane = pl.ds(pl.multiple_of(g * BLK, BLK), BLK)
        h = feat.astype(F32)
        stack[lane, 0:CH] = feat
        for m in range(3):
            stack[lane, (m + 1) * CH:(m + 2) * CH] = (cols[:, m:m + 1] * h).astype(BF16)

    tile(jnp.int32(0), True)
    stack_tile(jnp.int32(OWN), feat_ref[0, 0])

    @pl.loop(1, GHOSTS)
    def _(p):
        g = lax.rem(p + OWN, GHOSTS)
        pos_copy(8 - g).wait_recv()
        tile(p, False)

    @pl.loop(1, GHOSTS)
    def _(p):
        g = lax.rem(p + OWN, GHOSTS)
        feat_copy(8 - g).wait_recv()
        stack_tile(g, gfeat[g])

    def halves(nb):
        return jnp.dot(basis[...], stack[:, nb * 2 * CH:(nb + 1) * 2 * CH], preferred_element_type=F32)

    def weigh(values, row):
        total = None
        for k in range(NRAD):
            term = rad_ref[row, k:k + 1, :] * values[k * BLK:(k + 1) * BLK]
            total = term if total is None else total + term
        return total

    first_half = halves(0)
    sum_zero = weigh(first_half[:, :CH], 0)
    sum_one = weigh(first_half[:, :CH], 1)
    moment = [weigh(first_half[:, CH:], 1)]
    second_half = halves(1)
    moment.append(weigh(second_half[:, :CH], 1))
    moment.append(weigh(second_half[:, CH:], 1))

    first_bf = sum_zero.astype(BF16)
    second = [(moment[m] - own_c[m] * sum_one).astype(BF16) for m in range(3)]
    second_all = jnp.concatenate(second, axis=0)
    quadratic = jnp.dot(second_all, square_ref[...], preferred_element_type=F32)
    quad = [quadratic[m * BLK:(m + 1) * BLK] for m in range(3)]
    second_f = [s.astype(F32) for s in second]
    linear = jnp.dot(first_bf, mix_ref[...], preferred_element_type=F32)
    square_sum = quad[0] * second_f[0] + quad[1] * second_f[1] + quad[2] * second_f[2]
    updated_ref[0, 0] = (linear + square_sum).astype(BF16)
    cot_f = cot.astype(F32)
    weighted = jnp.concatenate([(cot_f * s).astype(BF16) for s in second_f], axis=0)
    through = lax.dot_general(weighted, square_ref[...], nt, preferred_element_type=F32)
    grad_second = [cot_f * quad[m] + through[m * BLK:(m + 1) * BLK] for m in range(3)]
    grad_one = -(own_c[0] * grad_second[0] + own_c[1] * grad_second[1] + own_c[2] * grad_second[2])
    for k in range(NRAD):
        rows = slice(k * BLK, (k + 1) * BLK)
        w0 = rad_ref[0, k:k + 1, :]
        w1 = rad_ref[1, k:k + 1, :]
        gbasis[rows, 0:CH] = (w0 * grad_first + w1 * grad_one).astype(BF16)
        for m in range(3):
            gbasis[rows, (m + 1) * CH:(m + 2) * CH] = (w1 * grad_second[m]).astype(BF16)

    def pull(g):
        lane = pl.ds(pl.multiple_of(g * BLK, BLK), BLK)
        pulled = jnp.dot(basis_t[lane, :], gbasis[...], preferred_element_type=F32)
        cols = gcols[g]
        total = pulled[:, 0:CH]
        for m in range(3):
            total = total + cols[:, m:m + 1] * pulled[:, (m + 1) * CH:(m + 2) * CH]
        return total

    @pl.loop(1, GHOSTS)
    def _(p):
        g = lax.rem(p + OWN, GHOSTS)
        out_grad[g] = pull(g).astype(BF16)
        grad_copy(g).start()

    total = pull(jnp.int32(OWN))
    for g in others:
        grad_copy(8 - g).wait_recv()
        total = total + in_grad[g].astype(F32)
    grad_ref[0, 0] = total
    for g in others:
        pos_copy(g).wait_send()
        feat_copy(g).wait_send()
        grad_copy(g).wait_send()


def solution(mesh):
    nx, ny = mesh.shape["gx"], mesh.shape["gy"]

    def body(positions, features, senders, counts, radial_w, mix_w, square_w, cotangent):
        vmem = pl.BlockSpec(memory_space=pltpu.VMEM)
        smem = pl.BlockSpec(memory_space=pltpu.SMEM)
        return pl.pallas_call(
            functools.partial(kernel, nx, ny),
            out_shape=(
                jax.ShapeDtypeStruct(features.shape, BF16),
                jax.ShapeDtypeStruct(features.shape, F32),
            ),
            in_specs=[vmem, vmem, smem, smem, vmem, vmem, vmem, vmem],
            out_specs=(vmem, vmem),
            scratch_shapes=[
                pltpu.VMEM((GHOSTS, 3, BLK), BF16),
                pltpu.VMEM((GHOSTS, BLK, CH), BF16),
                pltpu.VMEM((NRAD * BLK, GHOSTS * BLK), BF16),
                pltpu.VMEM((GHOSTS * BLK, NRAD * BLK), BF16),
                pltpu.VMEM((GHOSTS * BLK, 4 * CH), BF16),
                pltpu.VMEM((NRAD * BLK, 4 * CH), BF16),
                pltpu.VMEM((GHOSTS, BLK, BLK), F32),
                pltpu.VMEM((GHOSTS, BLK, CH), BF16),
                pltpu.VMEM((GHOSTS, BLK, CH), BF16),
            ] + [pltpu.SemaphoreType.DMA((GHOSTS,))] * 6,
            compiler_params=pltpu.CompilerParams(collective_id=0, has_side_effects=True),
            name="layer",
        )(positions, features, senders, counts, radial_w, mix_w, square_w, cotangent)

    placed = (
        P("gx", "gy", None, None),
        P("gx", "gy", None, None),
        P("gx", "gy", None, None),
        P("gx", "gy", None),
        P(),
        P(),
        P(),
        P("gx", "gy", None, None),
    )
    return jax.shard_map(
        body,
        mesh=mesh,
        in_specs=placed,
        out_specs=(P("gx", "gy", None, None), P("gx", "gy", None, None)),
        check_vma=False,
    )
```

```python
import functools
import math

import jax
import jax.numpy as jnp
from jax import lax
from jax.experimental import pallas as pl
from jax.experimental.pallas import tpu as pltpu
from jax.sharding import PartitionSpec as P

MESH = pl.DeviceIdType.MESH
BLK = 128
CH = 128
NRAD = 8
GHOSTS = 9
F32 = jnp.float32
BF16 = jnp.bfloat16
NT = (((1,), (1,)), ((), ()))

SERIES = [(-1.0) ** (n + 1) * math.pi ** (2 * n + 1) / math.factorial(2 * n + 1) for n in range(7)]

DX = [0, -1, 1]
DY = [0, 1, -1]


def mirrored(p):
    r, q = p // 3, p % 3
    return 3 * ((3 - r) % 3) + (3 - q) % 3


def radial(dx, dy, dz, keep):
    dist = jnp.sqrt(dx * dx + dy * dy + dz * dz)
    u = jnp.minimum(dist, 1.0)
    one_minus = 1.0 - u
    value = one_minus * one_minus * keep
    v = u - 0.5
    v2 = v * v
    acc = jnp.full_like(v2, SERIES[6])
    for coef in SERIES[5::-1]:
        acc = acc * v2 + coef
    cosine = acc * v
    twice = cosine + cosine
    out = [value, value * cosine]
    for _ in range(NRAD - 2):
        out.append(twice * out[-1] - out[-2])
    return [b.astype(BF16) for b in out]


def flipped(block):
    return block.astype(F32).T.astype(BF16)


def kernel(
    nx, ny,
    pos_hbm, feat_hbm, senders_hbm, counts_hbm, rad_hbm, mix_hbm, square_hbm, cot_hbm,
    updated_ref, grad_ref,
    pos, feat, senders, counts, rad, mix, square, cot,
    gpos, stack, basis, rows, gbasis, far_pos, far_feat, out_grad, in_grad,
    weight, own_col, cot_t, mix_t, square_t, grad_first, sums,
    local, psend, precv, fsend, frecv, gsend, grecv, far_precv, far_frecv, relay_psend, relay_fsend, ready,
):
    gx = lax.axis_index("gx")
    gy = lax.axis_index("gy")
    half = ny // 2
    is_down = (gy == 0) | (gy == half)
    is_up = (gy == half - 1) | (gy == ny - 1)

    def cell(dx, dy):
        return (lax.rem(gx + dx + nx, nx), lax.rem(gy + dy + ny, ny))

    def peer(p):
        return cell(DX[p % 3], DY[p // 3])

    loads = [
        pltpu.make_async_copy(src, dst, local.at[n])
        for n, (src, dst) in enumerate([
            (feat_hbm, feat), (pos_hbm, pos), (cot_hbm, cot), (rad_hbm, rad),
            (mix_hbm, mix), (square_hbm, square), (senders_hbm, senders), (counts_hbm, counts),
        ])
    ]
    for load in loads:
        load.start()

    barrier = pltpu.get_barrier_semaphore()

    def announce(device):
        pl.semaphore_signal(barrier, inc=1, device_id=device, device_id_type=MESH)

    for p in range(1, 3):
        announce(peer(p))
    for p in range(3, 6):
        @pl.when(jnp.logical_not(is_up))
        def _():
            announce(peer(p))
    for p in range(6, 9):
        announce(peer(p))

        @pl.when(is_down)
        def _():
            announce(cell(DX[p % 3], half))

    @pl.when(is_down)
    def _():
        announce(cell(0, half - 1))

    loads[0].wait()
    own_feat = flipped(feat[0, 0])
    stack[0, 0:CH, :] = own_feat
    loads[1].wait()
    pl.semaphore_wait(barrier, 8 + jnp.where(is_up, 1, 0))

    @pl.when(is_up)
    def _():
        pl.semaphore_signal(ready, inc=1, device_id=cell(0, 1 - half), device_id_type=MESH)

    def pos_copy(p):
        return pltpu.make_async_remote_copy(
            src_ref=pos.at[0, 0], dst_ref=gpos.at[mirrored(p)], send_sem=psend.at[p],
            recv_sem=precv.at[mirrored(p)], device_id=peer(p), device_id_type=MESH)

    def feat_copy(p):
        return pltpu.make_async_remote_copy(
            src_ref=stack.at[0, pl.ds(0, CH)], dst_ref=stack.at[mirrored(p), pl.ds(0, CH)], send_sem=fsend.at[p],
            recv_sem=frecv.at[mirrored(p)], device_id=peer(p), device_id_type=MESH)

    def far_copy(kind, q):
        there = (3 - q) % 3
        if kind == 0:
            return pltpu.make_async_remote_copy(
                src_ref=pos.at[0, 0], dst_ref=far_pos.at[there], send_sem=psend.at[6 + q],
                recv_sem=far_precv.at[there], device_id=cell(DX[q], half), device_id_type=MESH)
        return pltpu.make_async_remote_copy(
            src_ref=stack.at[0, pl.ds(0, CH)], dst_ref=far_feat.at[there], send_sem=fsend.at[6 + q],
            recv_sem=far_frecv.at[there], device_id=cell(DX[q], half), device_id_type=MESH)

    def relay_copy(kind, q):
        if kind == 0:
            return pltpu.make_async_remote_copy(
                src_ref=far_pos.at[q], dst_ref=gpos.at[3 + q], send_sem=relay_psend.at[q],
                recv_sem=precv.at[3 + q], device_id=cell(0, half - 1), device_id_type=MESH)
        return pltpu.make_async_remote_copy(
            src_ref=far_feat.at[q], dst_ref=stack.at[3 + q, pl.ds(0, CH)], send_sem=relay_fsend.at[q],
            recv_sem=frecv.at[3 + q], device_id=cell(0, half - 1), device_id_type=MESH)

    def pos_arrival(p):
        pltpu.make_async_remote_copy(
            src_ref=pos.at[0, 0], dst_ref=gpos.at[p], send_sem=psend.at[p],
            recv_sem=precv.at[p], device_id=peer(1), device_id_type=MESH).wait_recv()

    def feat_arrival(p):
        pltpu.make_async_remote_copy(
            src_ref=stack.at[0, pl.ds(0, CH)], dst_ref=stack.at[p, pl.ds(0, CH)], send_sem=fsend.at[p],
            recv_sem=frecv.at[p], device_id=peer(1), device_id_type=MESH).wait_recv()

    def grad_copy(p):
        return pltpu.make_async_remote_copy(
            src_ref=out_grad.at[p], dst_ref=in_grad.at[mirrored(p)], send_sem=gsend.at[p],
            recv_sem=grecv.at[mirrored(p)], device_id=peer(p), device_id_type=MESH)

    for kind in range(2):
        for p in (3, 4, 5, 6, 7, 8, 1, 2):
            direct = (pos_copy, feat_copy)[kind]
            if p < 6:
                direct(p).start()
            else:
                @pl.when(is_down)
                def _():
                    far_copy(kind, p - 6).start()

                @pl.when(jnp.logical_not(is_down))
                def _():
                    direct(p).start()

    own_rows = pos[0, 0].astype(F32)
    own_x = [own_rows[m:m + 1, :] for m in range(3)]
    columns = jnp.concatenate([own_rows, jnp.zeros((BLK - 3, BLK), F32)], axis=0).T
    for m in range(3):
        own_col[m] = jnp.broadcast_to(columns[:, m:m + 1], (BLK, BLK))
    for load in loads[2:]:
        load.wait()
    count = counts[0, 0, 0]
    radial_rows = jnp.concatenate([rad[0], rad[1], jnp.zeros((BLK - 2 * NRAD, CH), F32)], axis=0).T
    for n in range(2 * NRAD):
        weight[n] = jnp.broadcast_to(radial_rows[:, n:n + 1], (CH, BLK))
    cot_t[...] = flipped(cot[0, 0])
    mix_t[...] = flipped(mix[...])
    square_t[...] = flipped(square[...])
    grad_first[...] = jnp.dot(mix[...], cot_t[...], preferred_element_type=F32)
    diagonal = lax.broadcasted_iota(jnp.int32, (BLK, BLK), 0) == lax.broadcasted_iota(jnp.int32, (BLK, BLK), 1)

    def tile_basis(p, own):
        dx = lax.rem(2 * lax.rem(p, 3) + 1, 3) - 1
        dy = lax.rem(lax.div(p, 3) + 1, 3) - 1
        g = 3 * (dx + 1) + dy + 1
        live = jnp.int32(0)
        for t in range(8):
            live = live + jnp.where((senders[0, 0, 0, t] == g) & (t < count), 1, 0)
        keep = jnp.full((BLK, BLK), live.astype(F32))
        if own:
            keep = jnp.where(diagonal, 0.0, keep)
        axis_of = lax.broadcasted_iota(jnp.int32, (3, BLK), 0)
        shift = jnp.where(axis_of == 0, dx.astype(F32), jnp.where(axis_of == 1, dy.astype(F32), 0.0))
        place = (pos[0, 0] if own else gpos[p]).astype(F32) + shift
        for m in range(3):
            rows[p, m:m + 1, :] = place[m:m + 1, :]
        offsets = [place[m:m + 1, :] - own_col[m] for m in range(3)]
        for k, b in enumerate(radial(*offsets, keep)):
            basis[p, k * BLK:(k + 1) * BLK, :] = b

    def tile_stack(p):
        h = stack[p, 0:CH, :].astype(F32)
        for m in range(3):
            stack[p, (m + 1) * CH:(m + 2) * CH, :] = (rows[p, m:m + 1, :] * h).astype(BF16)

    def gather(first, last):
        left = jnp.concatenate([stack[p] for p in range(first, last)], axis=1)
        for pair in range(NRAD // 2):
            span = slice(2 * pair * BLK, 2 * (pair + 1) * BLK)
            right = jnp.concatenate([basis[p, span, :] for p in range(first, last)], axis=1)
            product = lax.dot_general(left, right, NT, preferred_element_type=F32)
            for n in range(5):
                block = max(n - 1, 0)
                part = product[block * CH:(block + 1) * CH]
                w = 0 if n == 0 else NRAD
                term = weight[w + 2 * pair] * part[:, :BLK] + weight[w + 2 * pair + 1] * part[:, BLK:]
                if first == 0 and pair == 0:
                    sums[n] = term
                else:
                    sums[n] += term

    tile_basis(jnp.int32(0), True)
    tile_stack(0)

    def receive(first, last):
        @pl.loop(first, last)
        def _(p):
            pos_arrival(p)
            tile_basis(p, False)

        @pl.loop(first, last)
        def _(p):
            feat_arrival(p)
            tile_stack(p)

    receive(1, 6)
    gather(0, 6)

    @pl.when(is_down)
    def _():
        for kind in range(2):
            for q in range(3):
                far_copy(kind, q).wait_recv()
        pl.semaphore_wait(ready, 1)
        for kind in range(2):
            for q in range(3):
                relay_copy(kind, q).start()

    receive(6, 9)
    gather(6, 9)

    sum_one = sums[1]
    second = [(sums[2 + m] - own_x[m] * sum_one).astype(BF16) for m in range(3)]
    quadratic = jnp.dot(square_t[...], jnp.concatenate(second, axis=1), preferred_element_type=F32)
    quad = [quadratic[:, m * BLK:(m + 1) * BLK] for m in range(3)]
    second_f = [s.astype(F32) for s in second]
    cot_f = cot_t[...].astype(F32)
    weighted = jnp.concatenate([(cot_f * s).astype(BF16) for s in second_f], axis=1)
    through = jnp.dot(square[...], weighted, preferred_element_type=F32)
    grad_second = [cot_f * quad[m] + through[:, m * BLK:(m + 1) * BLK] for m in range(3)]
    grad_one = -(own_x[0] * grad_second[0] + own_x[1] * grad_second[1] + own_x[2] * grad_second[2])
    for k in range(NRAD):
        lanes = slice(k * BLK, (k + 1) * BLK)
        w0, w1 = weight[k], weight[NRAD + k]
        gbasis[0:CH, lanes] = (w0 * grad_first[...] + w1 * grad_one).astype(BF16)
        for m in range(3):
            gbasis[(m + 1) * CH:(m + 2) * CH, lanes] = (w1 * grad_second[m]).astype(BF16)

    def pull(blocks):
        right = jnp.concatenate([basis[p] for p in blocks], axis=1)
        pulled = jnp.dot(gbasis[...], right, preferred_element_type=F32)
        out = []
        for n, p in enumerate(blocks):
            lanes = slice(n * BLK, (n + 1) * BLK)
            total = pulled[0:CH, lanes]
            for m in range(3):
                total = total + rows[p, m:m + 1, :] * pulled[(m + 1) * CH:(m + 2) * CH, lanes]
            out.append(total)
        return out

    for blocks in ((3, 4), (5, 1), (2, 6), (7, 8)):
        for p, total in zip(blocks, pull(blocks)):
            out_grad[p] = total.astype(BF16)
            grad_copy(p).start()

    linear = jnp.dot(mix_t[...], sums[0].astype(BF16), preferred_element_type=F32)
    square_sum = quad[0] * second_f[0] + quad[1] * second_f[1] + quad[2] * second_f[2]
    updated_ref[0, 0] = (linear + square_sum).T.astype(BF16)

    total = pull((0,))[0]
    for p in (1, 2, 3, 4, 5, 6, 7, 8):
        grad_copy(mirrored(p)).wait_recv()
        total = total + in_grad[p].astype(F32)
    grad_ref[0, 0] = total.T
    for p in range(1, GHOSTS):
        pos_copy(p).wait_send()
        feat_copy(p).wait_send()
        grad_copy(p).wait_send()

    @pl.when(is_down)
    def _():
        for kind in range(2):
            for q in range(3):
                relay_copy(kind, q).wait_send()


def solution(mesh):
    nx, ny = mesh.shape["gx"], mesh.shape["gy"]

    def body(positions, features, senders, counts, radial_w, mix_w, square_w, cotangent):
        vmem = pl.BlockSpec(memory_space=pltpu.VMEM)
        hbm = pl.BlockSpec(memory_space=pl.ANY)
        dma = pltpu.SemaphoreType.DMA
        return pl.pallas_call(
            functools.partial(kernel, nx, ny),
            out_shape=(
                jax.ShapeDtypeStruct(features.shape, BF16),
                jax.ShapeDtypeStruct(features.shape, F32),
            ),
            in_specs=[hbm] * 8,
            out_specs=(vmem, vmem),
            scratch_shapes=[
                pltpu.VMEM(positions.shape, BF16),
                pltpu.VMEM(features.shape, BF16),
                pltpu.SMEM(senders.shape, jnp.int32),
                pltpu.SMEM(counts.shape, jnp.int32),
                pltpu.VMEM(radial_w.shape, F32),
                pltpu.VMEM(mix_w.shape, BF16),
                pltpu.VMEM(square_w.shape, BF16),
                pltpu.VMEM(cotangent.shape, BF16),
                pltpu.VMEM((GHOSTS, 3, BLK), BF16),
                pltpu.VMEM((GHOSTS, 4 * CH, BLK), BF16),
                pltpu.VMEM((GHOSTS, NRAD * BLK, BLK), BF16),
                pltpu.VMEM((GHOSTS, 8, BLK), F32),
                pltpu.VMEM((4 * CH, NRAD * BLK), BF16),
                pltpu.VMEM((3, 3, BLK), BF16),
                pltpu.VMEM((3, CH, BLK), BF16),
                pltpu.VMEM((GHOSTS, CH, BLK), BF16),
                pltpu.VMEM((GHOSTS, CH, BLK), BF16),
                pltpu.VMEM((2 * NRAD, CH, BLK), F32),
                pltpu.VMEM((3, BLK, BLK), F32),
                pltpu.VMEM((CH, BLK), BF16),
                pltpu.VMEM((CH, CH), BF16),
                pltpu.VMEM((CH, CH), BF16),
                pltpu.VMEM((CH, BLK), F32),
                pltpu.VMEM((5, CH, BLK), F32),
                dma((8,)),
                dma((GHOSTS,)), dma((GHOSTS,)), dma((GHOSTS,)), dma((GHOSTS,)), dma((GHOSTS,)), dma((GHOSTS,)),
                dma((3,)), dma((3,)), dma((3,)), dma((3,)),
                pltpu.SemaphoreType.REGULAR,
            ],
            compiler_params=pltpu.CompilerParams(collective_id=0, has_side_effects=True),
            name="layer",
        )(positions, features, senders, counts, radial_w, mix_w, square_w, cotangent)

    placed = (
        P("gx", "gy", None, None),
        P("gx", "gy", None, None),
        P("gx", "gy", None, None),
        P("gx", "gy", None),
        P(),
        P(),
        P(),
        P("gx", "gy", None, None),
    )
    return jax.shard_map(
        body,
        mesh=mesh,
        in_specs=placed,
        out_specs=(P("gx", "gy", None, None), P("gx", "gy", None, None)),
        check_vma=False,
    )
```

```python
import functools
import math

import jax
import jax.numpy as jnp
from jax import lax
from jax.experimental import pallas as pl
from jax.experimental.pallas import tpu as pltpu
from jax.sharding import PartitionSpec as P

MESH = pl.DeviceIdType.MESH
BLK = 128
CH = 128
NRAD = 8
GHOSTS = 9
F32 = jnp.float32
BF16 = jnp.bfloat16
NT = (((1,), (1,)), ((), ()))

SERIES = [(-1.0) ** (n + 1) * math.pi ** (2 * n + 1) / math.factorial(2 * n + 1) for n in range(7)]

DX = [0, -1, 1]


def radial(dx, dy, dz, keep):
    dist = jnp.sqrt(dx * dx + dy * dy + dz * dz)
    u = jnp.minimum(dist, 1.0)
    one_minus = 1.0 - u
    value = one_minus * one_minus * keep
    v = u - 0.5
    v2 = v * v
    acc = jnp.full_like(v2, SERIES[6])
    for coef in SERIES[5::-1]:
        acc = acc * v2 + coef
    cosine = acc * v
    twice = cosine + cosine
    out = [value, value * cosine]
    for _ in range(NRAD - 2):
        out.append(twice * out[-1] - out[-2])
    return [b.astype(BF16) for b in out]


def flipped(block):
    return block.astype(F32).T.astype(BF16)


def kernel(
    nx, ny,
    pos_hbm, feat_hbm, senders_hbm, counts_hbm, rad_hbm, mix_hbm, square_hbm, cot_hbm,
    updated_ref, grad_ref,
    pos, feat, senders, counts, rad, mix, square, cot,
    gpos, stack, basis, rows, gbasis, far_pos, far_feat, out_grad, in_grad,
    weight, own_col, cot_t, mix_t, square_t, grad_first, sums,
    local, psend, precv, fsend, frecv, gsend, grecv, far_precv, far_frecv, ready,
):
    gx = lax.axis_index("gx")
    gy = lax.axis_index("gy")
    half = ny // 2
    is_down = (gy == 0) | (gy == half)
    is_up = (gy == half - 1) | (gy == ny - 1)

    sign = jnp.where(is_up, -1, 1)

    def cell(dx, dy):
        return (lax.rem(gx + dx + nx, nx), lax.rem(gy + dy + ny, ny))

    def step_y(r):
        return jnp.where(r == 0, 0, jnp.where(r == 1, sign, -sign))

    def peer(r, q):
        return cell(DX[q], step_y(r))

    def mirrored(r, q):
        dy = step_y(r)
        there = lax.rem(gy + dy + ny, ny)
        sign_there = jnp.where((there == half - 1) | (there == ny - 1), -1, 1)
        return 3 * jnp.where(dy == 0, 0, jnp.where(dy == -sign_there, 1, 2)) + (3 - q) % 3

    loads = [
        pltpu.make_async_copy(src, dst, local.at[n])
        for n, src, dst in (
            (0, feat_hbm, feat), (1, pos_hbm, pos), (2, cot_hbm, cot), (2, mix_hbm, mix), (2, square_hbm, square),
            (3, rad_hbm, rad), (4, senders_hbm, senders), (5, counts_hbm, counts))
    ]
    for load in loads:
        load.start()

    barrier = pltpu.get_barrier_semaphore()

    def announce(device):
        pl.semaphore_signal(barrier, inc=1, device_id=device, device_id_type=MESH)

    for r, q in ((0, 1), (0, 2), (1, 0), (1, 1), (1, 2)):
        announce(peer(r, q))
    for q in range(3):
        @pl.when(jnp.logical_not(is_up))
        def _():
            announce(peer(2, q))

        @pl.when(is_down)
        def _():
            announce(cell(DX[q], half))

    @pl.when(is_down)
    def _():
        announce(cell(0, half - 1))

    loads[0].wait()
    own_feat = flipped(feat[0, 0])
    stack[0, 0:CH, :] = own_feat
    loads[1].wait()
    pl.semaphore_wait(barrier, 8 + jnp.where(is_up, 1, 0))

    @pl.when(is_up)
    def _():
        pl.semaphore_signal(ready, inc=1, device_id=cell(0, 1 - half), device_id_type=MESH)

    def halo_copy(kind, r, q):
        p, there = 3 * r + q, mirrored(r, q)
        if kind == 0:
            return pltpu.make_async_remote_copy(
                src_ref=pos.at[0, 0], dst_ref=gpos.at[there], send_sem=psend,
                recv_sem=precv.at[there // 6], device_id=peer(r, q), device_id_type=MESH)
        return pltpu.make_async_remote_copy(
            src_ref=stack.at[0, pl.ds(0, CH)], dst_ref=stack.at[there, pl.ds(0, CH)], send_sem=fsend,
            recv_sem=frecv.at[there], device_id=peer(r, q), device_id_type=MESH)

    def far_copy(kind, q):
        there = (3 - q) % 3
        if kind == 0:
            return pltpu.make_async_remote_copy(
                src_ref=pos.at[0, 0], dst_ref=far_pos.at[there], send_sem=psend,
                recv_sem=far_precv, device_id=cell(DX[q], half), device_id_type=MESH)
        return pltpu.make_async_remote_copy(
            src_ref=stack.at[0, pl.ds(0, CH)], dst_ref=far_feat.at[there], send_sem=fsend,
            recv_sem=far_frecv, device_id=cell(DX[q], half), device_id_type=MESH)

    def relay_copy(kind, q):
        if kind == 0:
            return pltpu.make_async_remote_copy(
                src_ref=far_pos.at[q], dst_ref=gpos.at[6 + q], send_sem=psend,
                recv_sem=precv.at[1], device_id=cell(0, half - 1), device_id_type=MESH)
        return pltpu.make_async_remote_copy(
            src_ref=far_feat.at[q], dst_ref=stack.at[6 + q, pl.ds(0, CH)], send_sem=fsend,
            recv_sem=frecv.at[6 + q], device_id=cell(0, half - 1), device_id_type=MESH)

    def sent(ref, sem):
        pltpu.make_async_remote_copy(
            src_ref=ref, dst_ref=ref, send_sem=sem, recv_sem=far_precv,
            device_id=peer(0, 1), device_id_type=MESH).wait_send()

    def arrived(ref, sem):
        pltpu.make_async_remote_copy(
            src_ref=ref, dst_ref=ref, send_sem=gsend, recv_sem=sem,
            device_id=peer(0, 1), device_id_type=MESH).wait_recv()

    def grad_copy(r, q):
        p, there = 3 * r + q, mirrored(r, q)
        return pltpu.make_async_remote_copy(
            src_ref=out_grad.at[p], dst_ref=in_grad.at[there], send_sem=gsend,
            recv_sem=grecv.at[there // 6], device_id=peer(r, q), device_id_type=MESH)

    for kind in range(2):
        for q in range(3):
            @pl.when(is_down)
            def _():
                far_copy(kind, q).start()

            @pl.when(jnp.logical_not(is_down))
            def _():
                halo_copy(kind, 2, q).start()

        for r, q in ((1, 0), (1, 1), (1, 2), (0, 1), (0, 2)):
            halo_copy(kind, r, q).start()

    own_rows = pos[0, 0].astype(F32)
    own_x = [own_rows[m:m + 1, :] for m in range(3)]
    columns = jnp.concatenate([own_rows, jnp.zeros((BLK - 3, BLK), F32)], axis=0).T
    for m in range(3):
        own_col[m] = jnp.broadcast_to(columns[:, m:m + 1], (BLK, BLK))
    pltpu.make_async_copy(far_feat, far_feat, local.at[2]).wait()
    for load in loads[5:]:
        load.wait()
    count = counts[0, 0, 0]
    radial_rows = jnp.concatenate([rad[0], rad[1], jnp.zeros((BLK - 2 * NRAD, CH), F32)], axis=0).T
    for n in range(2 * NRAD):
        weight[n] = jnp.broadcast_to(radial_rows[:, n:n + 1], (CH, BLK))
    cot_t[...] = flipped(cot[0, 0])
    mix_t[...] = flipped(mix[...])
    square_t[...] = flipped(square[...])
    grad_first[...] = jnp.dot(mix[...], cot_t[...], preferred_element_type=F32)
    diagonal = lax.broadcasted_iota(jnp.int32, (BLK, BLK), 0) == lax.broadcasted_iota(jnp.int32, (BLK, BLK), 1)

    def tile_basis(p, own):
        dx = lax.rem(2 * lax.rem(p, 3) + 1, 3) - 1
        dy = step_y(lax.div(p, 3))
        g = 3 * (dx + 1) + dy + 1
        live = jnp.int32(0)
        for t in range(8):
            live = live + jnp.where((senders[0, 0, 0, t] == g) & (t < count), 1, 0)
        keep = jnp.full((BLK, BLK), live.astype(F32))
        if own:
            keep = jnp.where(diagonal, 0.0, keep)
        axis_of = lax.broadcasted_iota(jnp.int32, (3, BLK), 0)
        shift = jnp.where(axis_of == 0, dx.astype(F32), jnp.where(axis_of == 1, dy.astype(F32), 0.0))
        place = (pos[0, 0] if own else gpos[p]).astype(F32) + shift
        for m in range(3):
            rows[p, m:m + 1, :] = place[m:m + 1, :]
        offsets = [place[m:m + 1, :] - own_col[m] for m in range(3)]
        for k, b in enumerate(radial(*offsets, keep)):
            basis[p, k * BLK:(k + 1) * BLK, :] = b

    def tile_stack(p):
        h = stack[p, 0:CH, :].astype(F32)
        for m in range(3):
            stack[p, (m + 1) * CH:(m + 2) * CH, :] = (rows[p, m:m + 1, :] * h).astype(BF16)

    def gather(first, last):
        left = jnp.concatenate([stack[p] for p in range(first, last)], axis=1)
        for pair in range(NRAD // 2):
            span = slice(2 * pair * BLK, 2 * (pair + 1) * BLK)
            right = jnp.concatenate([basis[p, span, :] for p in range(first, last)], axis=1)
            product = lax.dot_general(left, right, NT, preferred_element_type=F32)
            for n in range(5):
                block = max(n - 1, 0)
                part = product[block * CH:(block + 1) * CH]
                w = 0 if n == 0 else NRAD
                term = weight[w + 2 * pair] * part[:, :BLK] + weight[w + 2 * pair + 1] * part[:, BLK:]
                if first == 0 and pair == 0:
                    sums[n] = term
                else:
                    sums[n] += term

    tile_basis(jnp.int32(0), True)
    tile_stack(0)

    def receive(first, last):
        arrived(gpos.at[pl.ds(first, last - first)], precv.at[first // 6])

        @pl.loop(first, last)
        def _(p):
            tile_basis(p, False)

        @pl.loop(first, last)
        def _(p):
            arrived(stack.at[p, pl.ds(0, CH)], frecv.at[p])
            tile_stack(p)

    receive(1, 6)

    @pl.when(is_down)
    def _():
        arrived(far_pos, far_precv)
        arrived(far_feat, far_frecv)
        pl.semaphore_wait(ready, 1)
        for kind in range(2):
            for q in range(3):
                relay_copy(kind, q).start()

    gather(0, 6)
    receive(6, 9)
    gather(6, 9)

    sum_one = sums[1]
    second = [(sums[2 + m] - own_x[m] * sum_one).astype(BF16) for m in range(3)]
    quadratic = jnp.dot(square_t[...], jnp.concatenate(second, axis=1), preferred_element_type=F32)
    quad = [quadratic[:, m * BLK:(m + 1) * BLK] for m in range(3)]
    second_f = [s.astype(F32) for s in second]
    cot_f = cot_t[...].astype(F32)
    weighted = jnp.concatenate([(cot_f * s).astype(BF16) for s in second_f], axis=1)
    through = jnp.dot(square[...], weighted, preferred_element_type=F32)
    grad_second = [cot_f * quad[m] + through[:, m * BLK:(m + 1) * BLK] for m in range(3)]
    grad_one = -(own_x[0] * grad_second[0] + own_x[1] * grad_second[1] + own_x[2] * grad_second[2])
    for k in range(NRAD):
        lanes = slice(k * BLK, (k + 1) * BLK)
        w0, w1 = weight[k], weight[NRAD + k]
        gbasis[0:CH, lanes] = (w0 * grad_first[...] + w1 * grad_one).astype(BF16)
        for m in range(3):
            gbasis[(m + 1) * CH:(m + 2) * CH, lanes] = (w1 * grad_second[m]).astype(BF16)

    def pull(blocks):
        right = jnp.concatenate([basis[p] for p in blocks], axis=1)
        pulled = jnp.dot(gbasis[...], right, preferred_element_type=F32)
        out = []
        for n, p in enumerate(blocks):
            lanes = slice(n * BLK, (n + 1) * BLK)
            total = pulled[0:CH, lanes]
            for m in range(3):
                total = total + rows[p, m:m + 1, :] * pulled[(m + 1) * CH:(m + 2) * CH, lanes]
            out.append(total)
        return out

    first = jnp.where(is_up, 2, 1)
    for n, r in enumerate((first, 3 - first)):
        blocks = [(r, 0), (r, 1), (r, 2), (0, n + 1)]
        totals = pull([3 * row + q for row, q in blocks])
        for (row, q), total in zip(blocks, totals):
            out_grad[3 * row + q] = total.astype(BF16)
        for row, q in blocks:
            grad_copy(row, q).start()

    linear = jnp.dot(mix_t[...], sums[0].astype(BF16), preferred_element_type=F32)
    square_sum = quad[0] * second_f[0] + quad[1] * second_f[1] + quad[2] * second_f[2]
    updated_ref[0, 0] = (linear + square_sum).T.astype(BF16)
    total = pull((0,))[0]
    for first, last in ((1, 6), (6, 9)):
        arrived(in_grad.at[pl.ds(first, last - first)], grecv.at[first // 6])
        for p in range(first, last):
            total = total + in_grad[p].astype(F32)
    grad_ref[0, 0] = total.T
    sent(gpos.at[pl.ds(1, 8)], psend)
    sent(in_grad.at[pl.ds(1, 8)], fsend)
    sent(in_grad.at[pl.ds(1, 8)], gsend)

    @pl.when(is_down)
    def _():
        sent(far_pos, psend)
        sent(far_feat, fsend)


def solution(mesh):
    nx, ny = mesh.shape["gx"], mesh.shape["gy"]

    def body(positions, features, senders, counts, radial_w, mix_w, square_w, cotangent):
        hbm = pl.BlockSpec(memory_space=pltpu.HBM)
        dma = pltpu.SemaphoreType.DMA
        vmem = pl.BlockSpec(memory_space=pltpu.VMEM)
        return pl.pallas_call(
            functools.partial(kernel, nx, ny),
            out_shape=(pltpu.VMEM(features.shape, BF16), pltpu.VMEM(features.shape, F32)),
            in_specs=[hbm] * 8,
            out_specs=(vmem, vmem),
            scratch_shapes=[
                pltpu.VMEM(positions.shape, BF16),
                pltpu.VMEM(features.shape, BF16),
                pltpu.SMEM(senders.shape, jnp.int32),
                pltpu.SMEM(counts.shape, jnp.int32),
                pltpu.VMEM(radial_w.shape, F32),
                pltpu.VMEM(mix_w.shape, BF16),
                pltpu.VMEM(square_w.shape, BF16),
                pltpu.VMEM(cotangent.shape, BF16),
                pltpu.VMEM((GHOSTS, 3, BLK), BF16),
                pltpu.VMEM((GHOSTS, 4 * CH, BLK), BF16),
                pltpu.VMEM((GHOSTS, NRAD * BLK, BLK), BF16),
                pltpu.VMEM((GHOSTS, 8, BLK), F32),
                pltpu.VMEM((4 * CH, NRAD * BLK), BF16),
                pltpu.VMEM((3, 3, BLK), BF16),
                pltpu.VMEM((3, CH, BLK), BF16),
                pltpu.VMEM((GHOSTS, CH, BLK), BF16),
                pltpu.VMEM((GHOSTS, CH, BLK), BF16),
                pltpu.VMEM((2 * NRAD, CH, BLK), F32),
                pltpu.VMEM((3, BLK, BLK), F32),
                pltpu.VMEM((CH, BLK), BF16),
                pltpu.VMEM((CH, CH), BF16),
                pltpu.VMEM((CH, CH), BF16),
                pltpu.VMEM((CH, BLK), F32),
                pltpu.VMEM((5, CH, BLK), F32),
                dma((6,)),
                dma, dma((2,)), dma, dma((GHOSTS,)), dma, dma((2,)),
                dma, dma,
                pltpu.SemaphoreType.REGULAR,
            ],
            compiler_params=pltpu.CompilerParams(collective_id=0, has_side_effects=True),
            name="layer",
        )(positions, features, senders, counts, radial_w, mix_w, square_w, cotangent)

    placed = (
        P("gx", "gy", None, None),
        P("gx", "gy", None, None),
        P("gx", "gy", None, None),
        P("gx", "gy", None),
        P(),
        P(),
        P(),
        P("gx", "gy", None, None),
    )
    return jax.shard_map(
        body,
        mesh=mesh,
        in_specs=placed,
        out_specs=(P("gx", "gy", None, None), P("gx", "gy", None, None)),
        check_vma=False,
    )
```

```python
import functools
import math

import jax
import jax.numpy as jnp
from jax import lax
from jax.experimental import pallas as pl
from jax.experimental.pallas import tpu as pltpu
from jax.sharding import PartitionSpec as P

MESH = pl.DeviceIdType.MESH
BLK = 128
CH = 128
NRAD = 8
GHOSTS = 9
F32 = jnp.float32
BF16 = jnp.bfloat16
NT = (((1,), (1,)), ((), ()))

SERIES = [(-1.0) ** (n + 1) * math.pi ** (2 * n + 1) / math.factorial(2 * n + 1) for n in range(7)]

DX = [0, -1, 1]


def radial(dx, dy, dz, keep):
    dist = jnp.sqrt(dx * dx + dy * dy + dz * dz)
    u = jnp.minimum(dist, 1.0)
    one_minus = 1.0 - u
    value = one_minus * one_minus * keep
    v = u - 0.5
    v2 = v * v
    acc = jnp.full_like(v2, SERIES[6])
    for coef in SERIES[5::-1]:
        acc = acc * v2 + coef
    cosine = acc * v
    twice = cosine + cosine
    out = [value, value * cosine]
    for _ in range(NRAD - 2):
        out.append(twice * out[-1] - out[-2])
    return [b.astype(BF16) for b in out]


def flipped(block):
    return block.astype(F32).T.astype(BF16)


def kernel(
    nx, ny,
    pos_hbm, feat_hbm, senders_hbm, counts_hbm, rad_hbm, mix_hbm, square_hbm, cot_hbm,
    updated_ref, grad_ref,
    pos, feat, senders, counts, rad, mix, square, cot,
    gpos, stack, basis, rows, gbasis, far_pos, far_feat, out_grad, in_grad,
    weight, own_col, cot_t, mix_t, square_t, grad_first, sums,
    local, psend, precv, fsend, frecv, gsend, grecv, far_precv, far_frecv, ready,
):
    gx = lax.axis_index("gx")
    gy = lax.axis_index("gy")
    half = ny // 2
    is_down = (gy == 0) | (gy == half)
    is_up = (gy == half - 1) | (gy == ny - 1)

    sign = jnp.where(is_up, -1, 1)

    def cell(dx, dy):
        return (lax.rem(gx + dx + nx, nx), lax.rem(gy + dy + ny, ny))

    def step_y(r):
        return jnp.where(r == 0, 0, jnp.where(r == 1, sign, -sign))

    def peer(r, q):
        return cell(DX[q], step_y(r))

    def mirrored(r, q):
        dy = step_y(r)
        there = lax.rem(gy + dy + ny, ny)
        sign_there = jnp.where((there == half - 1) | (there == ny - 1), -1, 1)
        return 3 * jnp.where(dy == 0, 0, jnp.where(dy == -sign_there, 1, 2)) + (3 - q) % 3

    loads = [
        pltpu.make_async_copy(src, dst, local.at[n])
        for n, src, dst in (
            (0, feat_hbm, feat), (1, pos_hbm, pos), (2, cot_hbm, cot), (2, mix_hbm, mix), (2, square_hbm, square),
            (3, rad_hbm, rad), (4, senders_hbm, senders), (5, counts_hbm, counts))
    ]
    for load in loads:
        load.start()

    barrier = pltpu.get_barrier_semaphore()

    def announce(device):
        pl.semaphore_signal(barrier, inc=1, device_id=device, device_id_type=MESH)

    for r, q in ((0, 1), (0, 2), (1, 0), (1, 1), (1, 2)):
        announce(peer(r, q))
    for q in range(3):
        @pl.when(jnp.logical_not(is_up))
        def _():
            announce(peer(2, q))

        @pl.when(is_down)
        def _():
            announce(cell(DX[q], half))

    @pl.when(is_down)
    def _():
        announce(cell(0, half - 1))

    loads[0].wait()
    own_feat = flipped(feat[0, 0])
    stack[0, 0:CH, :] = own_feat
    loads[1].wait()
    pl.semaphore_wait(barrier, 8 + jnp.where(is_up, 1, 0))

    @pl.when(is_up)
    def _():
        pl.semaphore_signal(ready, inc=1, device_id=cell(0, 1 - half), device_id_type=MESH)

    def halo_copy(kind, r, q):
        p, there = 3 * r + q, mirrored(r, q)
        if kind == 0:
            return pltpu.make_async_remote_copy(
                src_ref=pos.at[0, 0], dst_ref=gpos.at[there], send_sem=psend,
                recv_sem=precv.at[there // 6], device_id=peer(r, q), device_id_type=MESH)
        return pltpu.make_async_remote_copy(
            src_ref=stack.at[0, pl.ds(0, CH)], dst_ref=stack.at[there, pl.ds(0, CH)], send_sem=fsend,
            recv_sem=frecv.at[there], device_id=peer(r, q), device_id_type=MESH)

    def far_copy(kind, q):
        there = (3 - q) % 3
        if kind == 0:
            return pltpu.make_async_remote_copy(
                src_ref=pos.at[0, 0], dst_ref=far_pos.at[there], send_sem=psend,
                recv_sem=far_precv, device_id=cell(DX[q], half), device_id_type=MESH)
        return pltpu.make_async_remote_copy(
            src_ref=stack.at[0, pl.ds(0, CH)], dst_ref=far_feat.at[there], send_sem=fsend,
            recv_sem=far_frecv, device_id=cell(DX[q], half), device_id_type=MESH)

    def relay_copy(kind, q):
        if kind == 0:
            return pltpu.make_async_remote_copy(
                src_ref=far_pos.at[q], dst_ref=gpos.at[6 + q], send_sem=psend,
                recv_sem=precv.at[1], device_id=cell(0, half - 1), device_id_type=MESH)
        return pltpu.make_async_remote_copy(
            src_ref=far_feat.at[q], dst_ref=stack.at[6 + q, pl.ds(0, CH)], send_sem=fsend,
            recv_sem=frecv.at[6 + q], device_id=cell(0, half - 1), device_id_type=MESH)

    def sent(ref, sem):
        pltpu.make_async_remote_copy(
            src_ref=ref, dst_ref=ref, send_sem=sem, recv_sem=far_precv,
            device_id=peer(0, 1), device_id_type=MESH).wait_send()

    def arrived(ref, sem):
        pltpu.make_async_remote_copy(
            src_ref=ref, dst_ref=ref, send_sem=gsend, recv_sem=sem,
            device_id=peer(0, 1), device_id_type=MESH).wait_recv()

    def grad_copy(r, q):
        p, there = 3 * r + q, mirrored(r, q)
        return pltpu.make_async_remote_copy(
            src_ref=out_grad.at[p], dst_ref=in_grad.at[there], send_sem=gsend,
            recv_sem=grecv.at[there // 6], device_id=peer(r, q), device_id_type=MESH)

    for kind in range(2):
        @pl.when(is_up)
        def _():
            for r, q in ((2, 0), (0, 1), (0, 2), (2, 1), (2, 2), (1, 1), (1, 2), (1, 0)):
                halo_copy(kind, r, q).start()

        @pl.when(is_down)
        def _():
            for q in (1, 2, 0):
                far_copy(kind, q).start()

        @pl.when(jnp.logical_not(is_up))
        def _():
            for r, q in ((1, 1), (1, 2), (1, 0), (0, 1), (0, 2)):
                halo_copy(kind, r, q).start()

        @pl.when(jnp.logical_not(is_up | is_down))
        def _():
            for q in (1, 2, 0):
                halo_copy(kind, 2, q).start()

    own_rows = pos[0, 0].astype(F32)
    own_x = [own_rows[m:m + 1, :] for m in range(3)]
    columns = jnp.concatenate([own_rows, jnp.zeros((BLK - 3, BLK), F32)], axis=0).T
    for m in range(3):
        own_col[m] = jnp.broadcast_to(columns[:, m:m + 1], (BLK, BLK))
    pltpu.make_async_copy(far_feat, far_feat, local.at[2]).wait()
    for load in loads[5:]:
        load.wait()
    count = counts[0, 0, 0]
    radial_rows = jnp.concatenate([rad[0], rad[1], jnp.zeros((BLK - 2 * NRAD, CH), F32)], axis=0).T
    for n in range(2 * NRAD):
        weight[n] = jnp.broadcast_to(radial_rows[:, n:n + 1], (CH, BLK))
    cot_t[...] = flipped(cot[0, 0])
    mix_t[...] = flipped(mix[...])
    square_t[...] = flipped(square[...])
    grad_first[...] = jnp.dot(mix[...], cot_t[...], preferred_element_type=F32)
    diagonal = lax.broadcasted_iota(jnp.int32, (BLK, BLK), 0) == lax.broadcasted_iota(jnp.int32, (BLK, BLK), 1)

    def tile_basis(p, own):
        dx = lax.rem(2 * lax.rem(p, 3) + 1, 3) - 1
        dy = step_y(lax.div(p, 3))
        g = 3 * (dx + 1) + dy + 1
        live = jnp.int32(0)
        for t in range(8):
            live = live + jnp.where((senders[0, 0, 0, t] == g) & (t < count), 1, 0)
        keep = jnp.full((BLK, BLK), live.astype(F32))
        if own:
            keep = jnp.where(diagonal, 0.0, keep)
        axis_of = lax.broadcasted_iota(jnp.int32, (3, BLK), 0)
        shift = jnp.where(axis_of == 0, dx.astype(F32), jnp.where(axis_of == 1, dy.astype(F32), 0.0))
        place = (pos[0, 0] if own else gpos[p]).astype(F32) + shift
        for m in range(3):
            rows[p, m:m + 1, :] = place[m:m + 1, :]
        offsets = [place[m:m + 1, :] - own_col[m] for m in range(3)]
        for k, b in enumerate(radial(*offsets, keep)):
            basis[p, k * BLK:(k + 1) * BLK, :] = b

    def tile_stack(p):
        h = stack[p, 0:CH, :].astype(F32)
        for m in range(3):
            stack[p, (m + 1) * CH:(m + 2) * CH, :] = (rows[p, m:m + 1, :] * h).astype(BF16)

    def gather(first, last):
        left = jnp.concatenate([stack[p] for p in range(first, last)], axis=1)
        for pair in range(NRAD // 2):
            span = slice(2 * pair * BLK, 2 * (pair + 1) * BLK)
            right = jnp.concatenate([basis[p, span, :] for p in range(first, last)], axis=1)
            product = lax.dot_general(left, right, NT, preferred_element_type=F32)
            for n in range(5):
                block = max(n - 1, 0)
                part = product[block * CH:(block + 1) * CH]
                w = 0 if n == 0 else NRAD
                term = weight[w + 2 * pair] * part[:, :BLK] + weight[w + 2 * pair + 1] * part[:, BLK:]
                if first == 0 and pair == 0:
                    sums[n] = term
                else:
                    sums[n] += term

    tile_basis(jnp.int32(0), True)
    tile_stack(0)

    def receive(first, last):
        arrived(gpos.at[pl.ds(first, last - first)], precv.at[first // 6])

        @pl.loop(first, last)
        def _(p):
            tile_basis(p, False)

        @pl.loop(first, last)
        def _(p):
            arrived(stack.at[p, pl.ds(0, CH)], frecv.at[p])
            tile_stack(p)

    receive(1, 6)

    @pl.when(is_down)
    def _():
        arrived(far_pos, far_precv)
        arrived(far_feat, far_frecv)
        pl.semaphore_wait(ready, 1)
        for kind in range(2):
            for q in range(3):
                relay_copy(kind, q).start()

    gather(0, 6)
    receive(6, 9)
    gather(6, 9)

    sum_one = sums[1]
    second = [(sums[2 + m] - own_x[m] * sum_one).astype(BF16) for m in range(3)]
    quadratic = jnp.dot(square_t[...], jnp.concatenate(second, axis=1), preferred_element_type=F32)
    quad = [quadratic[:, m * BLK:(m + 1) * BLK] for m in range(3)]
    second_f = [s.astype(F32) for s in second]
    cot_f = cot_t[...].astype(F32)
    weighted = jnp.concatenate([(cot_f * s).astype(BF16) for s in second_f], axis=1)
    through = jnp.dot(square[...], weighted, preferred_element_type=F32)
    grad_second = [cot_f * quad[m] + through[:, m * BLK:(m + 1) * BLK] for m in range(3)]
    grad_one = -(own_x[0] * grad_second[0] + own_x[1] * grad_second[1] + own_x[2] * grad_second[2])
    for k in range(NRAD):
        lanes = slice(k * BLK, (k + 1) * BLK)
        w0, w1 = weight[k], weight[NRAD + k]
        gbasis[0:CH, lanes] = (w0 * grad_first[...] + w1 * grad_one).astype(BF16)
        for m in range(3):
            gbasis[(m + 1) * CH:(m + 2) * CH, lanes] = (w1 * grad_second[m]).astype(BF16)

    def pull(blocks):
        right = jnp.concatenate([basis[p] for p in blocks], axis=1)
        pulled = jnp.dot(gbasis[...], right, preferred_element_type=F32)
        out = []
        for n, p in enumerate(blocks):
            lanes = slice(n * BLK, (n + 1) * BLK)
            total = pulled[0:CH, lanes]
            for m in range(3):
                total = total + rows[p, m:m + 1, :] * pulled[(m + 1) * CH:(m + 2) * CH, lanes]
            out.append(total)
        return out

    first = jnp.where(is_up, 2, 1)
    for n, r in enumerate((first, 3 - first)):
        blocks = [(r, 1), (r, 2), (r, 0), (0, n + 1)]
        totals = pull([3 * row + q for row, q in blocks])
        for (row, q), total in zip(blocks, totals):
            out_grad[3 * row + q] = total.astype(BF16)
        for row, q in blocks:
            grad_copy(row, q).start()

    linear = jnp.dot(mix_t[...], sums[0].astype(BF16), preferred_element_type=F32)
    square_sum = quad[0] * second_f[0] + quad[1] * second_f[1] + quad[2] * second_f[2]
    updated_ref[0, 0] = (linear + square_sum).T.astype(BF16)
    total = pull((0,))[0]
    for first, last in ((1, 6), (6, 9)):
        arrived(in_grad.at[pl.ds(first, last - first)], grecv.at[first // 6])
        for p in range(first, last):
            total = total + in_grad[p].astype(F32)
    grad_ref[0, 0] = total.T
    sent(gpos.at[pl.ds(1, 8)], psend)
    sent(in_grad.at[pl.ds(1, 8)], fsend)
    sent(in_grad.at[pl.ds(1, 8)], gsend)

    @pl.when(is_down)
    def _():
        sent(far_pos, psend)
        sent(far_feat, fsend)


def solution(mesh):
    nx, ny = mesh.shape["gx"], mesh.shape["gy"]

    def body(positions, features, senders, counts, radial_w, mix_w, square_w, cotangent):
        hbm = pl.BlockSpec(memory_space=pltpu.HBM)
        dma = pltpu.SemaphoreType.DMA
        vmem = pl.BlockSpec(memory_space=pltpu.VMEM)
        return pl.pallas_call(
            functools.partial(kernel, nx, ny),
            out_shape=(pltpu.VMEM(features.shape, BF16), pltpu.VMEM(features.shape, F32)),
            in_specs=[hbm] * 8,
            out_specs=(vmem, vmem),
            scratch_shapes=[
                pltpu.VMEM(positions.shape, BF16),
                pltpu.VMEM(features.shape, BF16),
                pltpu.SMEM(senders.shape, jnp.int32),
                pltpu.SMEM(counts.shape, jnp.int32),
                pltpu.VMEM(radial_w.shape, F32),
                pltpu.VMEM(mix_w.shape, BF16),
                pltpu.VMEM(square_w.shape, BF16),
                pltpu.VMEM(cotangent.shape, BF16),
                pltpu.VMEM((GHOSTS, 3, BLK), BF16),
                pltpu.VMEM((GHOSTS, 4 * CH, BLK), BF16),
                pltpu.VMEM((GHOSTS, NRAD * BLK, BLK), BF16),
                pltpu.VMEM((GHOSTS, 8, BLK), F32),
                pltpu.VMEM((4 * CH, NRAD * BLK), BF16),
                pltpu.VMEM((3, 3, BLK), BF16),
                pltpu.VMEM((3, CH, BLK), BF16),
                pltpu.VMEM((GHOSTS, CH, BLK), BF16),
                pltpu.VMEM((GHOSTS, CH, BLK), BF16),
                pltpu.VMEM((2 * NRAD, CH, BLK), F32),
                pltpu.VMEM((3, BLK, BLK), F32),
                pltpu.VMEM((CH, BLK), BF16),
                pltpu.VMEM((CH, CH), BF16),
                pltpu.VMEM((CH, CH), BF16),
                pltpu.VMEM((CH, BLK), F32),
                pltpu.VMEM((5, CH, BLK), F32),
                dma((6,)),
                dma, dma((2,)), dma, dma((GHOSTS,)), dma, dma((2,)),
                dma, dma,
                pltpu.SemaphoreType.REGULAR,
            ],
            compiler_params=pltpu.CompilerParams(collective_id=0, has_side_effects=True),
            name="layer",
        )(positions, features, senders, counts, radial_w, mix_w, square_w, cotangent)

    placed = (
        P("gx", "gy", None, None),
        P("gx", "gy", None, None),
        P("gx", "gy", None, None),
        P("gx", "gy", None),
        P(),
        P(),
        P(),
        P("gx", "gy", None, None),
    )
    return jax.shard_map(
        body,
        mesh=mesh,
        in_specs=placed,
        out_specs=(P("gx", "gy", None, None), P("gx", "gy", None, None)),
        check_vma=False,
    )
```

```python
import functools
import math

import jax
import jax.numpy as jnp
from jax import lax
from jax.experimental import pallas as pl
from jax.experimental.pallas import tpu as pltpu
from jax.sharding import PartitionSpec as P

MESH = pl.DeviceIdType.MESH
BLK = 128
CH = 128
NRAD = 8
GHOSTS = 9
F32 = jnp.float32
BF16 = jnp.bfloat16
NT = (((1,), (1,)), ((), ()))

SERIES = [(-1.0) ** (n + 1) * math.pi ** (2 * n + 1) / math.factorial(2 * n + 1) for n in range(7)]

DX = [0, -1, 1]


def radial(dx, dy, dz, keep):
    dist = jnp.sqrt(dx * dx + dy * dy + dz * dz)
    u = jnp.minimum(dist, 1.0)
    one_minus = 1.0 - u
    value = one_minus * one_minus * keep
    v = u - 0.5
    v2 = v * v
    acc = jnp.full_like(v2, SERIES[6])
    for coef in SERIES[5::-1]:
        acc = acc * v2 + coef
    cosine = acc * v
    twice = cosine + cosine
    out = [value, value * cosine]
    for _ in range(NRAD - 2):
        out.append(twice * out[-1] - out[-2])
    return [b.astype(BF16) for b in out]


def flipped(block):
    return block.astype(F32).T.astype(BF16)


def kernel(
    nx, ny,
    pos_hbm, feat_hbm, senders_hbm, counts_hbm, rad_hbm, mix_hbm, square_hbm, cot_hbm,
    updated_ref, grad_ref,
    pos, feat, senders, counts, rad, mix, square, cot,
    gpos, stack, basis, rows, gbasis, far_pos, far_feat, out_grad, in_grad,
    weight, own_col, cot_t, mix_t, square_t, grad_first, sums,
    local, psend, precv, fsend, frecv, gsend, grecv, far_precv, far_frecv, ready,
):
    gx = lax.axis_index("gx")
    gy = lax.axis_index("gy")
    half = ny // 2
    is_down = (gy == 0) | (gy == half)
    is_up = (gy == half - 1) | (gy == ny - 1)
    is_next = (gy == half - 2) | (gy == ny - 2)
    at_end = is_up & (lax.rem(gx, 4) == 3)
    near = jnp.where(lax.rem(gx, 4) == 0, 2, 1)

    sign = jnp.where(is_up, -1, 1)

    def cell(dx, dy):
        return (lax.rem(gx + dx + nx, nx), lax.rem(gy + dy + ny, ny))

    def step_y(r):
        return jnp.where(r == 0, 0, jnp.where(r == 1, sign, -sign))

    def peer(r, q):
        return cell(DX[q], step_y(r))

    def mirrored(r, q):
        dy = step_y(r)
        there = lax.rem(gy + dy + ny, ny)
        sign_there = jnp.where((there == half - 1) | (there == ny - 1), -1, 1)
        return 3 * jnp.where(dy == 0, 0, jnp.where(dy == -sign_there, 1, 2)) + (3 - q) % 3

    loads = [
        pltpu.make_async_copy(src, dst, local.at[n])
        for n, src, dst in (
            (0, feat_hbm, feat), (1, pos_hbm, pos), (2, cot_hbm, cot), (2, mix_hbm, mix), (2, square_hbm, square),
            (3, rad_hbm, rad), (4, senders_hbm, senders), (5, counts_hbm, counts))
    ]
    barrier = pltpu.get_barrier_semaphore()

    def announce(device):
        pl.semaphore_signal(barrier, inc=1, device_id=device, device_id_type=MESH)

    for r, q in ((0, 1), (0, 2), (1, 0), (1, 1), (1, 2)):
        announce(peer(r, q))
    for q in range(3):
        @pl.when(jnp.logical_not(is_up))
        def _():
            announce(peer(2, q))

        @pl.when(is_down)
        def _():
            announce(cell(DX[q], half))

    @pl.when(is_down)
    def _():
        announce(cell(0, half - 1))

    for load in loads:
        load.start()
    loads[0].wait()
    own_feat = flipped(feat[0, 0])
    stack[0, 0:CH, :] = own_feat
    loads[1].wait()
    pl.semaphore_wait(barrier, 8 + jnp.where(is_up, 1, 0))

    @pl.when(is_up)
    def _():
        pl.semaphore_signal(ready, inc=1, device_id=cell(0, 1 - half), device_id_type=MESH)

    def halo_copy(kind, r, q):
        p, there = 3 * r + q, mirrored(r, q)
        if kind == 0:
            return pltpu.make_async_remote_copy(
                src_ref=pos.at[0, 0], dst_ref=gpos.at[there], send_sem=psend,
                recv_sem=precv.at[there], device_id=peer(r, q), device_id_type=MESH)
        return pltpu.make_async_remote_copy(
            src_ref=stack.at[0, pl.ds(0, CH)], dst_ref=stack.at[there, pl.ds(0, CH)], send_sem=fsend,
            recv_sem=frecv.at[there], device_id=peer(r, q), device_id_type=MESH)

    def far_copy(kind, q):
        there = (3 - q) % 3
        if kind == 0:
            return pltpu.make_async_remote_copy(
                src_ref=pos.at[0, 0], dst_ref=far_pos.at[there], send_sem=psend,
                recv_sem=far_precv, device_id=cell(DX[q], half), device_id_type=MESH)
        return pltpu.make_async_remote_copy(
            src_ref=stack.at[0, pl.ds(0, CH)], dst_ref=far_feat.at[there], send_sem=fsend,
            recv_sem=far_frecv, device_id=cell(DX[q], half), device_id_type=MESH)

    def relay_copy(kind, q):
        if kind == 0:
            return pltpu.make_async_remote_copy(
                src_ref=far_pos.at[q], dst_ref=gpos.at[6 + q], send_sem=psend,
                recv_sem=precv.at[6 + q], device_id=cell(0, half - 1), device_id_type=MESH)
        return pltpu.make_async_remote_copy(
            src_ref=far_feat.at[q], dst_ref=stack.at[6 + q, pl.ds(0, CH)], send_sem=fsend,
            recv_sem=frecv.at[6 + q], device_id=cell(0, half - 1), device_id_type=MESH)

    def sent(ref, sem):
        pltpu.make_async_remote_copy(
            src_ref=ref, dst_ref=ref, send_sem=sem, recv_sem=far_precv,
            device_id=peer(0, 1), device_id_type=MESH).wait_send()

    def arrived(ref, sem):
        pltpu.make_async_remote_copy(
            src_ref=ref, dst_ref=ref, send_sem=gsend, recv_sem=sem,
            device_id=peer(0, 1), device_id_type=MESH).wait_recv()

    def grad_copy(r, q):
        p, there = 3 * r + q, mirrored(r, q)
        return pltpu.make_async_remote_copy(
            src_ref=out_grad.at[p], dst_ref=in_grad.at[there], send_sem=gsend,
            recv_sem=grecv.at[there // 6], device_id=peer(r, q), device_id_type=MESH)

    def start(kind, directions):
        for r, q in directions:
            halo_copy(kind, r, q).start()

    for kind in range(2):
        @pl.when(is_up)
        def _():
            start(kind, ((2, 1), (2, 2), (2, 0), (0, 1), (0, 2), (1, 0)))

        @pl.when(is_down)
        def _():
            for q in (1, 2, 0):
                far_copy(kind, q).start()

        @pl.when(jnp.logical_not(is_up))
        def _():
            start(kind, ((1, 1), (1, 2), (1, 0)))

        @pl.when(jnp.logical_not(is_up | is_next))
        def _():
            start(kind, ((0, 1), (0, 2)))

        @pl.when(jnp.logical_not(is_up | is_next | is_down))
        def _():
            start(kind, ((2, 1), (2, 2), (2, 0)))

    own_rows = pos[0, 0].astype(F32)
    own_x = [own_rows[m:m + 1, :] for m in range(3)]
    columns = jnp.concatenate([own_rows, jnp.zeros((BLK - 3, BLK), F32)], axis=0).T
    for m in range(3):
        own_col[m] = jnp.broadcast_to(columns[:, m:m + 1], (BLK, BLK))
    pltpu.make_async_copy(far_feat, far_feat, local.at[2]).wait()
    for load in loads[5:]:
        load.wait()
    count = counts[0, 0, 0]
    radial_rows = jnp.concatenate([rad[0], rad[1], jnp.zeros((BLK - 2 * NRAD, CH), F32)], axis=0).T
    for n in range(2 * NRAD):
        weight[n] = jnp.broadcast_to(radial_rows[:, n:n + 1], (CH, BLK))
    cot_t[...] = flipped(cot[0, 0])
    mix_t[...] = flipped(mix[...])
    square_t[...] = flipped(square[...])
    grad_first[...] = jnp.dot(mix[...], cot_t[...], preferred_element_type=F32)
    diagonal = lax.broadcasted_iota(jnp.int32, (BLK, BLK), 0) == lax.broadcasted_iota(jnp.int32, (BLK, BLK), 1)

    def tile_basis(p, own):
        dx = lax.rem(2 * lax.rem(p, 3) + 1, 3) - 1
        dy = step_y(lax.div(p, 3))
        g = 3 * (dx + 1) + dy + 1
        live = jnp.int32(0)
        for t in range(8):
            live = live + jnp.where((senders[0, 0, 0, t] == g) & (t < count), 1, 0)
        keep = jnp.full((BLK, BLK), live.astype(F32))
        if own:
            keep = jnp.where(diagonal, 0.0, keep)
        axis_of = lax.broadcasted_iota(jnp.int32, (3, BLK), 0)
        shift = jnp.where(axis_of == 0, dx.astype(F32), jnp.where(axis_of == 1, dy.astype(F32), 0.0))
        place = (pos[0, 0] if own else gpos[p]).astype(F32) + shift
        for m in range(3):
            rows[p, m:m + 1, :] = place[m:m + 1, :]
        offsets = [place[m:m + 1, :] - own_col[m] for m in range(3)]
        for k, b in enumerate(radial(*offsets, keep)):
            basis[p, k * BLK:(k + 1) * BLK, :] = b

    def tile_stack(p):
        h = stack[p, 0:CH, :].astype(F32)
        for m in range(3):
            stack[p, (m + 1) * CH:(m + 2) * CH, :] = (rows[p, m:m + 1, :] * h).astype(BF16)

    def gather(blocks, begin=False):
        left = jnp.concatenate([stack[p] for p in blocks], axis=1)
        for pair in range(NRAD // 2):
            span = slice(2 * pair * BLK, 2 * (pair + 1) * BLK)
            right = jnp.concatenate([basis[p, span, :] for p in blocks], axis=1)
            product = lax.dot_general(left, right, NT, preferred_element_type=F32)
            for n in range(5):
                block = max(n - 1, 0)
                part = product[block * CH:(block + 1) * CH]
                w = 0 if n == 0 else NRAD
                term = weight[w + 2 * pair] * part[:, :BLK] + weight[w + 2 * pair + 1] * part[:, BLK:]
                if begin and pair == 0:
                    sums[n] = term
                else:
                    sums[n] += term

    tile_basis(jnp.int32(0), True)
    tile_stack(0)

    def receive(count, number):
        @pl.loop(0, count)
        def _(n):
            p = number(n)
            arrived(gpos.at[p], precv.at[p])
            tile_basis(p, False)

        @pl.loop(0, count)
        def _(n):
            p = number(n)
            arrived(stack.at[p, pl.ds(0, CH)], frecv.at[p])
            tile_stack(p)

    receive(1, lambda n: n + 3)
    gather((0, 3), begin=True)

    for kind in range(2):
        @pl.when(is_up)
        def _():
            start(kind, ((1, 1), (1, 2)))

        @pl.when(is_next)
        def _():
            start(kind, ((0, 1), (0, 2), (2, 1), (2, 2), (2, 0)))

    later = 3 - near
    receive(2, lambda n: near + 3 * n)
    gather((near, near + 3))
    receive(2, lambda n: jnp.where(at_end, 6 + n, later + 3 * n))

    @pl.when(is_down)
    def _():
        arrived(far_pos, far_precv)
        arrived(far_feat, far_frecv)
        pl.semaphore_wait(ready, 1)
        for kind in range(2):
            for q in range(3):
                relay_copy(kind, q).start()

    gather((jnp.where(at_end, 6, later), jnp.where(at_end, 7, later + 3)))
    receive(3, lambda n: jnp.where(at_end, jnp.where(n == 0, 8, later + 3 * (n - 1)), 6 + n))
    gather([jnp.where(at_end, end, other) for end, other in ((8, 6), (later, 7), (later + 3, 8))])

    sum_one = sums[1]
    second = [(sums[2 + m] - own_x[m] * sum_one).astype(BF16) for m in range(3)]
    quadratic = jnp.dot(square_t[...], jnp.concatenate(second, axis=1), preferred_element_type=F32)
    quad = [quadratic[:, m * BLK:(m + 1) * BLK] for m in range(3)]
    second_f = [s.astype(F32) for s in second]
    cot_f = cot_t[...].astype(F32)
    weighted = jnp.concatenate([(cot_f * s).astype(BF16) for s in second_f], axis=1)
    through = jnp.dot(square[...], weighted, preferred_element_type=F32)
    grad_second = [cot_f * quad[m] + through[:, m * BLK:(m + 1) * BLK] for m in range(3)]
    grad_one = -(own_x[0] * grad_second[0] + own_x[1] * grad_second[1] + own_x[2] * grad_second[2])
    for k in range(NRAD):
        lanes = slice(k * BLK, (k + 1) * BLK)
        w0, w1 = weight[k], weight[NRAD + k]
        gbasis[0:CH, lanes] = (w0 * grad_first[...] + w1 * grad_one).astype(BF16)
        for m in range(3):
            gbasis[(m + 1) * CH:(m + 2) * CH, lanes] = (w1 * grad_second[m]).astype(BF16)

    def pull(blocks):
        right = jnp.concatenate([basis[p] for p in blocks], axis=1)
        halves = [
            jnp.dot(gbasis[2 * n * CH:2 * (n + 1) * CH, :], right, preferred_element_type=F32)
            for n in range(2)
        ]
        out = []
        for n, p in enumerate(blocks):
            lanes = slice(n * BLK, (n + 1) * BLK)
            part = [halves[m // 2][m % 2 * CH:(m % 2 + 1) * CH, lanes] for m in range(4)]
            total = part[0]
            for m in range(3):
                total = total + rows[p, m:m + 1, :] * part[m + 1]
            out.append(total)
        return out

    first = jnp.where(is_up, 2, 1)
    second_row = 3 - first
    for blocks in (
        ((first, 1), (first, 2)), ((first, 0), (0, 1)), ((second_row, 1), (second_row, 2)), ((second_row, 0), (0, 2))):
        totals = pull([3 * row + q for row, q in blocks])
        for (row, q), total in zip(blocks, totals):
            out_grad[3 * row + q] = total.astype(BF16)
        for row, q in blocks:
            grad_copy(row, q).start()

    linear = jnp.dot(mix_t[...], sums[0].astype(BF16), preferred_element_type=F32)
    square_sum = quad[0] * second_f[0] + quad[1] * second_f[1] + quad[2] * second_f[2]
    updated_ref[0] = linear.T
    updated_ref[1] = square_sum.T
    grad_ref[0] = pull((0,))[0].T
    total = None
    for first, last in ((1, 6), (6, 9)):
        arrived(in_grad.at[pl.ds(first, last - first)], grecv.at[first // 6])
        for p in range(first, last):
            came = in_grad[p].astype(F32)
            total = came if total is None else total + came
    grad_ref[1] = total.T
    sent(gpos.at[pl.ds(1, 8)], psend)
    sent(in_grad.at[pl.ds(1, 8)], fsend)
    sent(in_grad.at[pl.ds(1, 8)], gsend)

    @pl.when(is_down)
    def _():
        sent(far_pos, psend)
        sent(far_feat, fsend)


def solution(mesh):
    nx, ny = mesh.shape["gx"], mesh.shape["gy"]

    def body(positions, features, senders, counts, radial_w, mix_w, square_w, cotangent):
        hbm = pl.BlockSpec(memory_space=pltpu.HBM)
        dma = pltpu.SemaphoreType.DMA
        vmem = pl.BlockSpec(memory_space=pltpu.VMEM)
        parts = pl.pallas_call(
            functools.partial(kernel, nx, ny),
            out_shape=(pltpu.VMEM((2, BLK, CH), F32), pltpu.VMEM((2, BLK, CH), F32)),
            in_specs=[hbm] * 8,
            out_specs=(vmem, vmem),
            scratch_shapes=[
                pltpu.VMEM(positions.shape, BF16),
                pltpu.VMEM(features.shape, BF16),
                pltpu.SMEM(senders.shape, jnp.int32),
                pltpu.SMEM(counts.shape, jnp.int32),
                pltpu.VMEM(radial_w.shape, F32),
                pltpu.VMEM(mix_w.shape, BF16),
                pltpu.VMEM(square_w.shape, BF16),
                pltpu.VMEM(cotangent.shape, BF16),
                pltpu.VMEM((GHOSTS, 3, BLK), BF16),
                pltpu.VMEM((GHOSTS, 4 * CH, BLK), BF16),
                pltpu.VMEM((GHOSTS, NRAD * BLK, BLK), BF16),
                pltpu.VMEM((GHOSTS, 8, BLK), F32),
                pltpu.VMEM((4 * CH, NRAD * BLK), BF16),
                pltpu.VMEM((3, 3, BLK), BF16),
                pltpu.VMEM((3, CH, BLK), BF16),
                pltpu.VMEM((GHOSTS, CH, BLK), BF16),
                pltpu.VMEM((GHOSTS, CH, BLK), BF16),
                pltpu.VMEM((2 * NRAD, CH, BLK), F32),
                pltpu.VMEM((3, BLK, BLK), F32),
                pltpu.VMEM((CH, BLK), BF16),
                pltpu.VMEM((CH, CH), BF16),
                pltpu.VMEM((CH, CH), BF16),
                pltpu.VMEM((CH, BLK), F32),
                pltpu.VMEM((5, CH, BLK), F32),
                dma((6,)),
                dma, dma((GHOSTS,)), dma, dma((GHOSTS,)), dma, dma((2,)),
                dma, dma,
                pltpu.SemaphoreType.REGULAR,
            ],
            compiler_params=pltpu.CompilerParams(collective_id=0, has_side_effects=True),
            name="layer",
        )(positions, features, senders, counts, radial_w, mix_w, square_w, cotangent)
        updated, grad = lax.reduce(
            parts, (jnp.float32(0), jnp.float32(0)), lambda a, b: (a[0] + b[0], a[1] + b[1]), (0,))
        return updated.astype(BF16)[None, None], grad[None, None]

    placed = (
        P("gx", "gy", None, None),
        P("gx", "gy", None, None),
        P("gx", "gy", None, None),
        P("gx", "gy", None),
        P(),
        P(),
        P(),
        P("gx", "gy", None, None),
    )
    return jax.shard_map(
        body,
        mesh=mesh,
        in_specs=placed,
        out_specs=(P("gx", "gy", None, None), P("gx", "gy", None, None)),
        check_vma=False,
    )
```

```python
import functools
import math

import jax
import jax.numpy as jnp
from jax import lax
from jax.experimental import pallas as pl
from jax.experimental.pallas import tpu as pltpu
from jax.sharding import PartitionSpec as P

MESH = pl.DeviceIdType.MESH
BLK = 128
CH = 128
NRAD = 8
GHOSTS = 9
F32 = jnp.float32
BF16 = jnp.bfloat16
NT = (((1,), (1,)), ((), ()))

SERIES = [(-1.0) ** (n + 1) * math.pi ** (2 * n + 1) / math.factorial(2 * n + 1) for n in range(7)]

DX = [0, -1, 1]


def radial(dx, dy, dz, keep):
    dist = jnp.sqrt(dx * dx + dy * dy + dz * dz)
    u = jnp.minimum(dist, 1.0)
    one_minus = 1.0 - u
    value = one_minus * one_minus * keep
    v = u - 0.5
    v2 = v * v
    acc = jnp.full_like(v2, SERIES[6])
    for coef in SERIES[5::-1]:
        acc = acc * v2 + coef
    cosine = acc * v
    twice = cosine + cosine
    out = [value, value * cosine]
    for _ in range(NRAD - 2):
        out.append(twice * out[-1] - out[-2])
    return [b.astype(BF16) for b in out]


def flipped(block):
    return block.astype(F32).T.astype(BF16)


def kernel(
    nx, ny,
    pos_hbm, feat_hbm, senders_hbm, counts_hbm, rad_hbm, mix_hbm, square_hbm, cot_hbm,
    updated_ref, grad_ref,
    pos, feat, senders, counts, rad, mix, square, cot,
    gpos, stack, basis, rows, gbasis, far_pos, far_feat, out_grad, in_grad,
    weight, own_col, cot_t, mix_t, square_t, grad_first, sums,
    local, psend, precv, fsend, frecv, gsend, grecv, far_precv, far_frecv, ready,
):
    gx = lax.axis_index("gx")
    gy = lax.axis_index("gy")
    half = ny // 2
    is_down = (gy == 0) | (gy == half)
    is_up = (gy == half - 1) | (gy == ny - 1)
    is_next = (gy == half - 2) | (gy == ny - 2)
    at_end = is_up & (lax.rem(gx, 4) == 3)
    near = jnp.where(lax.rem(gx, 4) == 0, 2, 1)

    sign = jnp.where(is_up, -1, 1)

    def cell(dx, dy):
        return (lax.rem(gx + dx + nx, nx), lax.rem(gy + dy + ny, ny))

    def step_y(r):
        return jnp.where(r == 0, 0, jnp.where(r == 1, sign, -sign))

    def peer(r, q):
        return cell(DX[q], step_y(r))

    def mirrored(r, q):
        dy = step_y(r)
        there = lax.rem(gy + dy + ny, ny)
        sign_there = jnp.where((there == half - 1) | (there == ny - 1), -1, 1)
        return 3 * jnp.where(dy == 0, 0, jnp.where(dy == -sign_there, 1, 2)) + (3 - q) % 3

    loads = [
        pltpu.make_async_copy(src, dst, local.at[n])
        for n, src, dst in (
            (0, feat_hbm, feat), (1, pos_hbm, pos), (2, cot_hbm, cot), (2, mix_hbm, mix), (2, square_hbm, square),
            (3, rad_hbm, rad), (4, senders_hbm, senders), (5, counts_hbm, counts))
    ]
    barrier = pltpu.get_barrier_semaphore()

    def announce(device):
        pl.semaphore_signal(barrier, inc=1, device_id=device, device_id_type=MESH)

    for r, q in ((0, 1), (0, 2), (1, 0), (1, 1), (1, 2)):
        announce(peer(r, q))
    for q in range(3):
        @pl.when(jnp.logical_not(is_up))
        def _():
            announce(peer(2, q))

        @pl.when(is_down)
        def _():
            announce(cell(DX[q], half))

    @pl.when(is_down)
    def _():
        announce(cell(0, half - 1))

    for load in loads:
        load.start()
    loads[0].wait()
    own_feat = flipped(feat[0, 0])
    stack[0, 0:CH, :] = own_feat
    loads[1].wait()
    pl.semaphore_wait(barrier, 8 + jnp.where(is_up, 1, 0))

    @pl.when(is_up)
    def _():
        pl.semaphore_signal(ready, inc=1, device_id=cell(0, 1 - half), device_id_type=MESH)

    def halo_copy(kind, r, q):
        p, there = 3 * r + q, mirrored(r, q)
        if kind == 0:
            return pltpu.make_async_remote_copy(
                src_ref=pos.at[0, 0], dst_ref=gpos.at[there], send_sem=psend,
                recv_sem=precv.at[there], device_id=peer(r, q), device_id_type=MESH)
        return pltpu.make_async_remote_copy(
            src_ref=stack.at[0, pl.ds(0, CH)], dst_ref=stack.at[there, pl.ds(0, CH)], send_sem=fsend,
            recv_sem=frecv.at[there], device_id=peer(r, q), device_id_type=MESH)

    def far_copy(kind, q):
        there = (3 - q) % 3
        if kind == 0:
            return pltpu.make_async_remote_copy(
                src_ref=pos.at[0, 0], dst_ref=far_pos.at[there], send_sem=psend,
                recv_sem=far_precv, device_id=cell(DX[q], half), device_id_type=MESH)
        return pltpu.make_async_remote_copy(
            src_ref=stack.at[0, pl.ds(0, CH)], dst_ref=far_feat.at[there], send_sem=fsend,
            recv_sem=far_frecv, device_id=cell(DX[q], half), device_id_type=MESH)

    def relay_copy(kind, q):
        if kind == 0:
            return pltpu.make_async_remote_copy(
                src_ref=far_pos.at[q], dst_ref=gpos.at[6 + q], send_sem=psend,
                recv_sem=precv.at[6 + q], device_id=cell(0, half - 1), device_id_type=MESH)
        return pltpu.make_async_remote_copy(
            src_ref=far_feat.at[q], dst_ref=stack.at[6 + q, pl.ds(0, CH)], send_sem=fsend,
            recv_sem=frecv.at[6 + q], device_id=cell(0, half - 1), device_id_type=MESH)

    def sent(ref, sem):
        pltpu.make_async_remote_copy(
            src_ref=ref, dst_ref=ref, send_sem=sem, recv_sem=far_precv,
            device_id=peer(0, 1), device_id_type=MESH).wait_send()

    def arrived(ref, sem):
        pltpu.make_async_remote_copy(
            src_ref=ref, dst_ref=ref, send_sem=gsend, recv_sem=sem,
            device_id=peer(0, 1), device_id_type=MESH).wait_recv()

    def grad_copy(r, q):
        p, there = 3 * r + q, mirrored(r, q)
        return pltpu.make_async_remote_copy(
            src_ref=out_grad.at[p], dst_ref=in_grad.at[there], send_sem=gsend,
            recv_sem=grecv.at[there // 6], device_id=peer(r, q), device_id_type=MESH)

    def start(kind, directions):
        for r, q in directions:
            halo_copy(kind, r, q).start()

    for kind in range(2):
        @pl.when(is_up)
        def _():
            start(kind, ((2, 1), (2, 2), (2, 0), (0, 1), (0, 2), (1, 0)))

        @pl.when(is_down)
        def _():
            for q in (1, 2, 0):
                far_copy(kind, q).start()

        @pl.when(jnp.logical_not(is_up))
        def _():
            start(kind, ((1, 1), (1, 2), (1, 0)))

        @pl.when(jnp.logical_not(is_up | is_next))
        def _():
            start(kind, ((0, 1), (0, 2)))

        @pl.when(jnp.logical_not(is_up | is_next | is_down))
        def _():
            start(kind, ((2, 1), (2, 2), (2, 0)))

    own_rows = pos[0, 0].astype(F32)
    own_x = [own_rows[m:m + 1, :] for m in range(3)]
    columns = jnp.concatenate([own_rows, jnp.zeros((BLK - 3, BLK), F32)], axis=0).T
    for m in range(3):
        own_col[m] = jnp.broadcast_to(columns[:, m:m + 1], (BLK, BLK))
    pltpu.make_async_copy(far_feat, far_feat, local.at[2]).wait()
    for load in loads[5:]:
        load.wait()
    count = counts[0, 0, 0]
    radial_rows = jnp.concatenate([rad[0], rad[1], jnp.zeros((BLK - 2 * NRAD, CH), F32)], axis=0).T
    for n in range(2 * NRAD):
        weight[n] = jnp.broadcast_to(radial_rows[:, n:n + 1], (CH, BLK))
    cot_t[...] = flipped(cot[0, 0])
    mix_t[...] = flipped(mix[...])
    square_t[...] = flipped(square[...])
    grad_first[...] = jnp.dot(mix[...], cot_t[...], preferred_element_type=F32)
    diagonal = lax.broadcasted_iota(jnp.int32, (BLK, BLK), 0) == lax.broadcasted_iota(jnp.int32, (BLK, BLK), 1)

    def tile_basis(p, own):
        dx = lax.rem(2 * lax.rem(p, 3) + 1, 3) - 1
        dy = step_y(lax.div(p, 3))
        g = 3 * (dx + 1) + dy + 1
        live = jnp.int32(0)
        for t in range(8):
            live = live + jnp.where((senders[0, 0, 0, t] == g) & (t < count), 1, 0)
        keep = jnp.full((BLK, BLK), live.astype(F32))
        if own:
            keep = jnp.where(diagonal, 0.0, keep)
        axis_of = lax.broadcasted_iota(jnp.int32, (3, BLK), 0)
        shift = jnp.where(axis_of == 0, dx.astype(F32), jnp.where(axis_of == 1, dy.astype(F32), 0.0))
        place = (pos[0, 0] if own else gpos[p]).astype(F32) + shift
        for m in range(3):
            rows[p, m:m + 1, :] = place[m:m + 1, :]
        offsets = [place[m:m + 1, :] - own_col[m] for m in range(3)]
        for k, b in enumerate(radial(*offsets, keep)):
            basis[p, k * BLK:(k + 1) * BLK, :] = b

    def tile_stack(p):
        h = stack[p, 0:CH, :].astype(F32)
        for m in range(3):
            stack[p, (m + 1) * CH:(m + 2) * CH, :] = (rows[p, m:m + 1, :] * h).astype(BF16)

    def gather(blocks, begin=False):
        left = jnp.concatenate([stack[p] for p in blocks], axis=1)
        for pair in range(NRAD // 2):
            span = slice(2 * pair * BLK, 2 * (pair + 1) * BLK)
            right = jnp.concatenate([basis[p, span, :] for p in blocks], axis=1)
            product = lax.dot_general(left, right, NT, preferred_element_type=F32)
            for n in range(5):
                block = max(n - 1, 0)
                part = product[block * CH:(block + 1) * CH]
                w = 0 if n == 0 else NRAD
                term = weight[w + 2 * pair] * part[:, :BLK] + weight[w + 2 * pair + 1] * part[:, BLK:]
                if begin and pair == 0:
                    sums[n] = term
                else:
                    sums[n] += term

    tile_basis(jnp.int32(0), True)
    tile_stack(0)

    def receive(count, number):
        @pl.loop(0, count)
        def _(n):
            p = number(n)
            arrived(gpos.at[p], precv.at[p])
            tile_basis(p, False)

        @pl.loop(0, count)
        def _(n):
            p = number(n)
            arrived(stack.at[p, pl.ds(0, CH)], frecv.at[p])
            tile_stack(p)

    receive(1, lambda n: n + 3)
    gather((0, 3), begin=True)

    for kind in range(2):
        @pl.when(is_up)
        def _():
            start(kind, ((1, 1), (1, 2)))

        @pl.when(is_next)
        def _():
            start(kind, ((0, 1), (0, 2), (2, 1), (2, 2), (2, 0)))

    later = 3 - near
    receive(2, lambda n: near + 3 * n)
    gather((near, near + 3))
    receive(2, lambda n: jnp.where(at_end, 6 + n, later + 3 * n))

    @pl.when(is_down)
    def _():
        arrived(far_pos, far_precv)
        arrived(far_feat, far_frecv)
        pl.semaphore_wait(ready, 1)
        for kind in range(2):
            for q in range(3):
                relay_copy(kind, q).start()

    early = jnp.where(is_down & (gx == nx - 1), 8, jnp.where(is_down & (gx == 0), 7, 6))
    receive(1, lambda n: jnp.where(at_end, 8, early) + n)
    gather((jnp.where(at_end, 6, later), jnp.where(at_end, 7, later + 3), jnp.where(at_end, 8, early)))
    last = (
        jnp.where(at_end, later, jnp.where(early == 6, 7, 6)),
        jnp.where(at_end, later + 3, jnp.where(early == 8, 7, 8)),
    )
    receive(2, lambda n: jnp.where(n == 0, last[0], last[1]))
    gather(last)

    sum_one = sums[1]
    second = [(sums[2 + m] - own_x[m] * sum_one).astype(BF16) for m in range(3)]
    quadratic = jnp.dot(square_t[...], jnp.concatenate(second, axis=1), preferred_element_type=F32)
    quad = [quadratic[:, m * BLK:(m + 1) * BLK] for m in range(3)]
    second_f = [s.astype(F32) for s in second]
    cot_f = cot_t[...].astype(F32)
    weighted = jnp.concatenate([(cot_f * s).astype(BF16) for s in second_f], axis=1)
    through = jnp.dot(square[...], weighted, preferred_element_type=F32)
    grad_second = [cot_f * quad[m] + through[:, m * BLK:(m + 1) * BLK] for m in range(3)]
    grad_one = -(own_x[0] * grad_second[0] + own_x[1] * grad_second[1] + own_x[2] * grad_second[2])
    for k in range(NRAD):
        lanes = slice(k * BLK, (k + 1) * BLK)
        w0, w1 = weight[k], weight[NRAD + k]
        gbasis[0:CH, lanes] = (w0 * grad_first[...] + w1 * grad_one).astype(BF16)
        for m in range(3):
            gbasis[(m + 1) * CH:(m + 2) * CH, lanes] = (w1 * grad_second[m]).astype(BF16)

    def pull(blocks):
        right = jnp.concatenate([basis[p] for p in blocks], axis=1)
        halves = [
            jnp.dot(gbasis[2 * n * CH:2 * (n + 1) * CH, :], right, preferred_element_type=F32)
            for n in range(2)
        ]
        out = []
        for n, p in enumerate(blocks):
            lanes = slice(n * BLK, (n + 1) * BLK)
            part = [halves[m // 2][m % 2 * CH:(m % 2 + 1) * CH, lanes] for m in range(4)]
            total = part[0]
            for m in range(3):
                total = total + rows[p, m:m + 1, :] * part[m + 1]
            out.append(total)
        return out

    first = jnp.where(is_up, 2, 1)
    second_row = 3 - first
    for blocks in (
        ((first, 1), (first, 2)), ((first, 0), (0, 1)), ((second_row, 1), (second_row, 2)), ((second_row, 0), (0, 2))):
        totals = pull([3 * row + q for row, q in blocks])
        for (row, q), total in zip(blocks, totals):
            out_grad[3 * row + q] = total.astype(BF16)
        for row, q in blocks:
            grad_copy(row, q).start()

    linear = jnp.dot(mix_t[...], sums[0].astype(BF16), preferred_element_type=F32)
    square_sum = quad[0] * second_f[0] + quad[1] * second_f[1] + quad[2] * second_f[2]
    updated_ref[0] = linear.T
    updated_ref[1] = square_sum.T
    grad_ref[0] = pull((0,))[0].T
    total = None
    for first, last in ((1, 6), (6, 9)):
        arrived(in_grad.at[pl.ds(first, last - first)], grecv.at[first // 6])
        for p in range(first, last):
            came = in_grad[p].astype(F32)
            total = came if total is None else total + came
    grad_ref[1] = total.T
    sent(gpos.at[pl.ds(1, 8)], psend)
    sent(in_grad.at[pl.ds(1, 8)], fsend)
    sent(in_grad.at[pl.ds(1, 8)], gsend)

    @pl.when(is_down)
    def _():
        sent(far_pos, psend)
        sent(far_feat, fsend)


def solution(mesh):
    nx, ny = mesh.shape["gx"], mesh.shape["gy"]

    def body(positions, features, senders, counts, radial_w, mix_w, square_w, cotangent):
        hbm = pl.BlockSpec(memory_space=pltpu.HBM)
        dma = pltpu.SemaphoreType.DMA
        vmem = pl.BlockSpec(memory_space=pltpu.VMEM)
        parts = pl.pallas_call(
            functools.partial(kernel, nx, ny),
            out_shape=(pltpu.VMEM((2, BLK, CH), F32), pltpu.VMEM((2, BLK, CH), F32)),
            in_specs=[hbm] * 8,
            out_specs=(vmem, vmem),
            scratch_shapes=[
                pltpu.VMEM(positions.shape, BF16),
                pltpu.VMEM(features.shape, BF16),
                pltpu.SMEM(senders.shape, jnp.int32),
                pltpu.SMEM(counts.shape, jnp.int32),
                pltpu.VMEM(radial_w.shape, F32),
                pltpu.VMEM(mix_w.shape, BF16),
                pltpu.VMEM(square_w.shape, BF16),
                pltpu.VMEM(cotangent.shape, BF16),
                pltpu.VMEM((GHOSTS, 3, BLK), BF16),
                pltpu.VMEM((GHOSTS, 4 * CH, BLK), BF16),
                pltpu.VMEM((GHOSTS, NRAD * BLK, BLK), BF16),
                pltpu.VMEM((GHOSTS, 8, BLK), F32),
                pltpu.VMEM((4 * CH, NRAD * BLK), BF16),
                pltpu.VMEM((3, 3, BLK), BF16),
                pltpu.VMEM((3, CH, BLK), BF16),
                pltpu.VMEM((GHOSTS, CH, BLK), BF16),
                pltpu.VMEM((GHOSTS, CH, BLK), BF16),
                pltpu.VMEM((2 * NRAD, CH, BLK), F32),
                pltpu.VMEM((3, BLK, BLK), F32),
                pltpu.VMEM((CH, BLK), BF16),
                pltpu.VMEM((CH, CH), BF16),
                pltpu.VMEM((CH, CH), BF16),
                pltpu.VMEM((CH, BLK), F32),
                pltpu.VMEM((5, CH, BLK), F32),
                dma((6,)),
                dma, dma((GHOSTS,)), dma, dma((GHOSTS,)), dma, dma((2,)),
                dma, dma,
                pltpu.SemaphoreType.REGULAR,
            ],
            compiler_params=pltpu.CompilerParams(collective_id=0, has_side_effects=True),
            name="layer",
        )(positions, features, senders, counts, radial_w, mix_w, square_w, cotangent)
        updated, grad = lax.reduce(
            parts, (jnp.float32(0), jnp.float32(0)), lambda a, b: (a[0] + b[0], a[1] + b[1]), (0,))
        return updated.astype(BF16)[None, None], grad[None, None]

    placed = (
        P("gx", "gy", None, None),
        P("gx", "gy", None, None),
        P("gx", "gy", None, None),
        P("gx", "gy", None),
        P(),
        P(),
        P(),
        P("gx", "gy", None, None),
    )
    return jax.shard_map(
        body,
        mesh=mesh,
        in_specs=placed,
        out_specs=(P("gx", "gy", None, None), P("gx", "gy", None, None)),
        check_vma=False,
    )
```

```python
import functools
import math

import jax
import jax.numpy as jnp
from jax import lax
from jax.experimental import pallas as pl
from jax.experimental.pallas import tpu as pltpu
from jax.sharding import PartitionSpec as P

MESH = pl.DeviceIdType.MESH
BLK = 128
CH = 128
NRAD = 8
GHOSTS = 9
F32 = jnp.float32
BF16 = jnp.bfloat16
NT = (((1,), (1,)), ((), ()))

SERIES = [(-1.0) ** (n + 1) * math.pi ** (2 * n + 1) / math.factorial(2 * n + 1) for n in range(7)]

DX = [0, -1, 1]


def radial(dx, dy, dz, keep):
    dist = jnp.sqrt(dx * dx + dy * dy + dz * dz)
    u = jnp.minimum(dist, 1.0)
    one_minus = 1.0 - u
    value = one_minus * one_minus * keep
    v = u - 0.5
    v2 = v * v
    acc = jnp.full_like(v2, SERIES[6])
    for coef in SERIES[5::-1]:
        acc = acc * v2 + coef
    cosine = acc * v
    twice = cosine + cosine
    out = [value, value * cosine]
    for _ in range(NRAD - 2):
        out.append(twice * out[-1] - out[-2])
    return [b.astype(BF16) for b in out]


def flipped(block):
    return block.astype(F32).T.astype(BF16)


def kernel(
    nx, ny,
    pos_hbm, feat_hbm, senders_hbm, counts_hbm, rad_hbm, mix_hbm, square_hbm, cot_hbm,
    updated_ref, grad_ref,
    pos, feat, senders, counts, rad, mix, square, cot,
    gpos, stack, basis, rows, gbasis, far_pos, far_feat, out_grad, in_grad,
    weight, own_col, cot_t, mix_t, square_t, grad_first, sums,
    local, psend, precv, fsend, frecv, gsend, grecv, far_precv, far_frecv, ready,
):
    gx = lax.axis_index("gx")
    gy = lax.axis_index("gy")
    half = ny // 2
    is_down = (gy == 0) | (gy == half)
    is_up = (gy == half - 1) | (gy == ny - 1)
    is_next = (gy == half - 2) | (gy == ny - 2)
    at_end = is_up & (lax.rem(gx, 4) == 3)
    near = jnp.where(lax.rem(gx, 4) == 0, 2, 1)

    sign = jnp.where(is_up, -1, 1)

    def cell(dx, dy):
        return (lax.rem(gx + dx + nx, nx), lax.rem(gy + dy + ny, ny))

    def step_y(r):
        return jnp.where(r == 0, 0, jnp.where(r == 1, sign, -sign))

    def peer(r, q):
        return cell(DX[q], step_y(r))

    def mirrored(r, q):
        dy = step_y(r)
        there = lax.rem(gy + dy + ny, ny)
        sign_there = jnp.where((there == half - 1) | (there == ny - 1), -1, 1)
        return 3 * jnp.where(dy == 0, 0, jnp.where(dy == -sign_there, 1, 2)) + (3 - q) % 3

    loads = [
        pltpu.make_async_copy(src, dst, local.at[n])
        for n, src, dst in (
            (0, feat_hbm, feat), (1, pos_hbm, pos), (2, cot_hbm, cot), (2, mix_hbm, mix), (2, square_hbm, square),
            (3, rad_hbm, rad), (4, senders_hbm, senders), (5, counts_hbm, counts))
    ]
    barrier = pltpu.get_barrier_semaphore()

    def announce(device):
        pl.semaphore_signal(barrier, inc=1, device_id=device, device_id_type=MESH)

    for r, q in ((0, 1), (0, 2), (1, 0), (1, 1), (1, 2)):
        announce(peer(r, q))
    for q in range(3):
        @pl.when(jnp.logical_not(is_up))
        def _():
            announce(peer(2, q))

        @pl.when(is_down)
        def _():
            announce(cell(DX[q], half))

    @pl.when(is_down)
    def _():
        announce(cell(0, half - 1))

    for load in loads:
        load.start()
    loads[0].wait()
    own_feat = flipped(feat[0, 0])
    stack[0, 0:CH, :] = own_feat
    loads[1].wait()
    pl.semaphore_wait(barrier, 8 + jnp.where(is_up, 1, 0))

    @pl.when(is_up)
    def _():
        pl.semaphore_signal(ready, inc=1, device_id=cell(0, 1 - half), device_id_type=MESH)

    def halo_copy(kind, r, q):
        p, there = 3 * r + q, mirrored(r, q)
        if kind == 0:
            return pltpu.make_async_remote_copy(
                src_ref=pos.at[0, 0], dst_ref=gpos.at[there], send_sem=psend,
                recv_sem=precv.at[there], device_id=peer(r, q), device_id_type=MESH)
        return pltpu.make_async_remote_copy(
            src_ref=stack.at[0, pl.ds(0, CH)], dst_ref=stack.at[there, pl.ds(0, CH)], send_sem=fsend,
            recv_sem=frecv.at[there], device_id=peer(r, q), device_id_type=MESH)

    def far_copy(kind, q):
        there = (3 - q) % 3
        if kind == 0:
            return pltpu.make_async_remote_copy(
                src_ref=pos.at[0, 0], dst_ref=far_pos.at[there], send_sem=psend,
                recv_sem=far_precv, device_id=cell(DX[q], half), device_id_type=MESH)
        return pltpu.make_async_remote_copy(
            src_ref=stack.at[0, pl.ds(0, CH)], dst_ref=far_feat.at[there], send_sem=fsend,
            recv_sem=far_frecv, device_id=cell(DX[q], half), device_id_type=MESH)

    def relay_copy(kind, q):
        if kind == 0:
            return pltpu.make_async_remote_copy(
                src_ref=far_pos.at[q], dst_ref=gpos.at[6 + q], send_sem=psend,
                recv_sem=precv.at[6 + q], device_id=cell(0, half - 1), device_id_type=MESH)
        return pltpu.make_async_remote_copy(
            src_ref=far_feat.at[q], dst_ref=stack.at[6 + q, pl.ds(0, CH)], send_sem=fsend,
            recv_sem=frecv.at[6 + q], device_id=cell(0, half - 1), device_id_type=MESH)

    def sent(ref, sem):
        pltpu.make_async_remote_copy(
            src_ref=ref, dst_ref=ref, send_sem=sem, recv_sem=far_precv,
            device_id=peer(0, 1), device_id_type=MESH).wait_send()

    def arrived(ref, sem):
        pltpu.make_async_remote_copy(
            src_ref=ref, dst_ref=ref, send_sem=gsend, recv_sem=sem,
            device_id=peer(0, 1), device_id_type=MESH).wait_recv()

    def grad_copy(r, q):
        p, there = 3 * r + q, mirrored(r, q)
        return pltpu.make_async_remote_copy(
            src_ref=out_grad.at[p], dst_ref=in_grad.at[there], send_sem=gsend,
            recv_sem=grecv.at[there // 6], device_id=peer(r, q), device_id_type=MESH)

    def start(kind, directions):
        for r, q in directions:
            halo_copy(kind, r, q).start()

    for kind in range(2):
        @pl.when(is_up)
        def _():
            start(kind, ((2, 1), (2, 2), (2, 0), (0, 1), (0, 2), (1, 0)))

        @pl.when(is_down)
        def _():
            for q in (1, 2, 0):
                far_copy(kind, q).start()

        @pl.when(jnp.logical_not(is_up))
        def _():
            start(kind, ((1, 1), (1, 2), (1, 0)))

        @pl.when(jnp.logical_not(is_up | is_next))
        def _():
            start(kind, ((0, 1), (0, 2)))

        @pl.when(jnp.logical_not(is_up | is_next | is_down))
        def _():
            start(kind, ((2, 1), (2, 2), (2, 0)))

    own_rows = pos[0, 0].astype(F32)
    own_x = [own_rows[m:m + 1, :] for m in range(3)]
    columns = jnp.concatenate([own_rows, jnp.zeros((BLK - 3, BLK), F32)], axis=0).T
    for m in range(3):
        own_col[m] = jnp.broadcast_to(columns[:, m:m + 1], (BLK, BLK))
    pltpu.make_async_copy(far_feat, far_feat, local.at[2]).wait()
    for load in loads[5:]:
        load.wait()
    count = counts[0, 0, 0]
    radial_rows = jnp.concatenate([rad[0], rad[1], jnp.zeros((BLK - 2 * NRAD, CH), F32)], axis=0).T
    for n in range(2 * NRAD):
        weight[n] = jnp.broadcast_to(radial_rows[:, n:n + 1], (CH, BLK))
    cot_t[...] = flipped(cot[0, 0])
    mix_t[...] = flipped(mix[...])
    square_t[...] = flipped(square[...])
    grad_first[...] = jnp.dot(mix[...], cot_t[...], preferred_element_type=F32)
    diagonal = lax.broadcasted_iota(jnp.int32, (BLK, BLK), 0) == lax.broadcasted_iota(jnp.int32, (BLK, BLK), 1)

    def tile_basis(p, own):
        dx = lax.rem(2 * lax.rem(p, 3) + 1, 3) - 1
        dy = step_y(lax.div(p, 3))
        g = 3 * (dx + 1) + dy + 1
        live = jnp.int32(0)
        for t in range(8):
            live = live + jnp.where((senders[0, 0, 0, t] == g) & (t < count), 1, 0)
        keep = jnp.full((BLK, BLK), live.astype(F32))
        if own:
            keep = jnp.where(diagonal, 0.0, keep)
        axis_of = lax.broadcasted_iota(jnp.int32, (3, BLK), 0)
        shift = jnp.where(axis_of == 0, dx.astype(F32), jnp.where(axis_of == 1, dy.astype(F32), 0.0))
        place = (pos[0, 0] if own else gpos[p]).astype(F32) + shift
        for m in range(3):
            rows[p, m:m + 1, :] = place[m:m + 1, :]
        offsets = [place[m:m + 1, :] - own_col[m] for m in range(3)]
        for k, b in enumerate(radial(*offsets, keep)):
            basis[p, k * BLK:(k + 1) * BLK, :] = b

    def tile_stack(p):
        h = stack[p, 0:CH, :].astype(F32)
        for m in range(3):
            stack[p, (m + 1) * CH:(m + 2) * CH, :] = (rows[p, m:m + 1, :] * h).astype(BF16)

    def gather(blocks, begin=False):
        left = jnp.concatenate([stack[p] for p in blocks], axis=1)
        for pair in range(NRAD // 2):
            span = slice(2 * pair * BLK, 2 * (pair + 1) * BLK)
            right = jnp.concatenate([basis[p, span, :] for p in blocks], axis=1)
            product = lax.dot_general(left, right, NT, preferred_element_type=F32)
            for n in range(5):
                block = max(n - 1, 0)
                part = product[block * CH:(block + 1) * CH]
                w = 0 if n == 0 else NRAD
                term = weight[w + 2 * pair] * part[:, :BLK] + weight[w + 2 * pair + 1] * part[:, BLK:]
                if begin and pair == 0:
                    sums[n] = term
                else:
                    sums[n] += term

    tile_basis(jnp.int32(0), True)
    tile_stack(0)

    def place(first, stop, number):
        @pl.loop(first, stop)
        def _(n):
            p = number(n)
            arrived(gpos.at[p], precv.at[p])
            tile_basis(p, False)

    def collect(first, stop, number):
        @pl.loop(first, stop)
        def _(n):
            p = number(n)
            arrived(stack.at[p, pl.ds(0, CH)], frecv.at[p])
            tile_stack(p)

    def receive(count, number):
        place(0, count, number)
        collect(0, count, number)

    receive(1, lambda n: n + 3)
    gather((0, 3), begin=True)

    for kind in range(2):
        @pl.when(is_up)
        def _():
            start(kind, ((1, 1), (1, 2)))

        @pl.when(is_next)
        def _():
            start(kind, ((0, 1), (0, 2), (2, 1), (2, 2), (2, 0)))

    later = 3 - near
    receive(2, lambda n: near + 3 * n)
    gather((near, near + 3))
    receive(2, lambda n: jnp.where(at_end, 6 + n, later + 3 * n))

    @pl.when(is_down)
    def _():
        arrived(far_pos, far_precv)
        arrived(far_feat, far_frecv)
        pl.semaphore_wait(ready, 1)
        for kind in range(2):
            for q in range(3):
                relay_copy(kind, q).start()

    early = jnp.where(is_down & (gx == nx - 1), 8, jnp.where(is_down & (gx == 0), 7, 6))
    middle = jnp.where(at_end, 8, early)
    last = (
        jnp.where(at_end, later, jnp.where(early == 6, 7, 6)),
        jnp.where(at_end, later + 3, jnp.where(early == 8, 7, 8)),
    )

    def order(n):
        return jnp.where(n == 0, middle, jnp.where(n == 1, last[0], last[1]))

    ahead = jnp.where(at_end, 1, 3)
    place(0, ahead, order)
    collect(0, 1, order)
    gather((jnp.where(at_end, 6, later), jnp.where(at_end, 7, later + 3), middle))
    place(ahead, 3, order)
    collect(1, 3, order)
    gather(last)

    sum_one = sums[1]
    second = [(sums[2 + m] - own_x[m] * sum_one).astype(BF16) for m in range(3)]
    quadratic = jnp.dot(square_t[...], jnp.concatenate(second, axis=1), preferred_element_type=F32)
    quad = [quadratic[:, m * BLK:(m + 1) * BLK] for m in range(3)]
    second_f = [s.astype(F32) for s in second]
    cot_f = cot_t[...].astype(F32)
    weighted = jnp.concatenate([(cot_f * s).astype(BF16) for s in second_f], axis=1)
    through = jnp.dot(square[...], weighted, preferred_element_type=F32)
    grad_second = [cot_f * quad[m] + through[:, m * BLK:(m + 1) * BLK] for m in range(3)]
    grad_one = -(own_x[0] * grad_second[0] + own_x[1] * grad_second[1] + own_x[2] * grad_second[2])
    for k in range(NRAD):
        lanes = slice(k * BLK, (k + 1) * BLK)
        w0, w1 = weight[k], weight[NRAD + k]
        gbasis[0:CH, lanes] = (w0 * grad_first[...] + w1 * grad_one).astype(BF16)
        for m in range(3):
            gbasis[(m + 1) * CH:(m + 2) * CH, lanes] = (w1 * grad_second[m]).astype(BF16)

    def pull(blocks):
        right = jnp.concatenate([basis[p] for p in blocks], axis=1)
        halves = [
            jnp.dot(gbasis[2 * n * CH:2 * (n + 1) * CH, :], right, preferred_element_type=F32)
            for n in range(2)
        ]
        out = []
        for n, p in enumerate(blocks):
            lanes = slice(n * BLK, (n + 1) * BLK)
            part = [halves[m // 2][m % 2 * CH:(m % 2 + 1) * CH, lanes] for m in range(4)]
            total = part[0]
            for m in range(3):
                total = total + rows[p, m:m + 1, :] * part[m + 1]
            out.append(total)
        return out

    first = jnp.where(is_up, 2, 1)
    second_row = 3 - first
    for blocks in (
        ((first, 1), (first, 2)), ((first, 0), (0, 1)), ((second_row, 1), (second_row, 2)), ((second_row, 0), (0, 2))):
        totals = pull([3 * row + q for row, q in blocks])
        for (row, q), total in zip(blocks, totals):
            out_grad[3 * row + q] = total.astype(BF16)
        for row, q in blocks:
            grad_copy(row, q).start()

    linear = jnp.dot(mix_t[...], sums[0].astype(BF16), preferred_element_type=F32)
    square_sum = quad[0] * second_f[0] + quad[1] * second_f[1] + quad[2] * second_f[2]
    updated_ref[0] = linear.T
    updated_ref[1] = square_sum.T
    grad_ref[0] = pull((0,))[0].T
    total = None
    for first, last in ((1, 6), (6, 9)):
        arrived(in_grad.at[pl.ds(first, last - first)], grecv.at[first // 6])
        for p in range(first, last):
            came = in_grad[p].astype(F32)
            total = came if total is None else total + came
    grad_ref[1] = total.T
    sent(gpos.at[pl.ds(1, 8)], psend)
    sent(in_grad.at[pl.ds(1, 8)], fsend)
    sent(in_grad.at[pl.ds(1, 8)], gsend)

    @pl.when(is_down)
    def _():
        sent(far_pos, psend)
        sent(far_feat, fsend)


def solution(mesh):
    nx, ny = mesh.shape["gx"], mesh.shape["gy"]

    def body(positions, features, senders, counts, radial_w, mix_w, square_w, cotangent):
        hbm = pl.BlockSpec(memory_space=pltpu.HBM)
        dma = pltpu.SemaphoreType.DMA
        vmem = pl.BlockSpec(memory_space=pltpu.VMEM)
        parts = pl.pallas_call(
            functools.partial(kernel, nx, ny),
            out_shape=(pltpu.VMEM((2, BLK, CH), F32), pltpu.VMEM((2, BLK, CH), F32)),
            in_specs=[hbm] * 8,
            out_specs=(vmem, vmem),
            scratch_shapes=[
                pltpu.VMEM(positions.shape, BF16),
                pltpu.VMEM(features.shape, BF16),
                pltpu.SMEM(senders.shape, jnp.int32),
                pltpu.SMEM(counts.shape, jnp.int32),
                pltpu.VMEM(radial_w.shape, F32),
                pltpu.VMEM(mix_w.shape, BF16),
                pltpu.VMEM(square_w.shape, BF16),
                pltpu.VMEM(cotangent.shape, BF16),
                pltpu.VMEM((GHOSTS, 3, BLK), BF16),
                pltpu.VMEM((GHOSTS, 4 * CH, BLK), BF16),
                pltpu.VMEM((GHOSTS, NRAD * BLK, BLK), BF16),
                pltpu.VMEM((GHOSTS, 8, BLK), F32),
                pltpu.VMEM((4 * CH, NRAD * BLK), BF16),
                pltpu.VMEM((3, 3, BLK), BF16),
                pltpu.VMEM((3, CH, BLK), BF16),
                pltpu.VMEM((GHOSTS, CH, BLK), BF16),
                pltpu.VMEM((GHOSTS, CH, BLK), BF16),
                pltpu.VMEM((2 * NRAD, CH, BLK), F32),
                pltpu.VMEM((3, BLK, BLK), F32),
                pltpu.VMEM((CH, BLK), BF16),
                pltpu.VMEM((CH, CH), BF16),
                pltpu.VMEM((CH, CH), BF16),
                pltpu.VMEM((CH, BLK), F32),
                pltpu.VMEM((5, CH, BLK), F32),
                dma((6,)),
                dma, dma((GHOSTS,)), dma, dma((GHOSTS,)), dma, dma((2,)),
                dma, dma,
                pltpu.SemaphoreType.REGULAR,
            ],
            compiler_params=pltpu.CompilerParams(collective_id=0, has_side_effects=True),
            name="layer",
        )(positions, features, senders, counts, radial_w, mix_w, square_w, cotangent)
        updated, grad = lax.reduce(
            parts, (jnp.float32(0), jnp.float32(0)), lambda a, b: (a[0] + b[0], a[1] + b[1]), (0,))
        return updated.astype(BF16)[None, None], grad[None, None]

    placed = (
        P("gx", "gy", None, None),
        P("gx", "gy", None, None),
        P("gx", "gy", None, None),
        P("gx", "gy", None),
        P(),
        P(),
        P(),
        P("gx", "gy", None, None),
    )
    return jax.shard_map(
        body,
        mesh=mesh,
        in_specs=placed,
        out_specs=(P("gx", "gy", None, None), P("gx", "gy", None, None)),
        check_vma=False,
    )
```

```python
import functools
import math

import jax
import jax.numpy as jnp
from jax import lax
from jax.experimental import pallas as pl
from jax.experimental.pallas import tpu as pltpu
from jax.sharding import PartitionSpec as P

MESH = pl.DeviceIdType.MESH
BLK = 128
CH = 128
NRAD = 8
GHOSTS = 9
F32 = jnp.float32
BF16 = jnp.bfloat16
NT = (((1,), (1,)), ((), ()))

SERIES = [(-1.0) ** (n + 1) * math.pi ** (2 * n + 1) / math.factorial(2 * n + 1) for n in range(7)]

DX = [0, -1, 1]


def radial(dx, dy, dz, keep):
    dist = jnp.sqrt(dx * dx + dy * dy + dz * dz)
    u = jnp.minimum(dist, 1.0)
    one_minus = 1.0 - u
    value = one_minus * one_minus * keep
    v = u - 0.5
    v2 = v * v
    acc = jnp.full_like(v2, SERIES[6])
    for coef in SERIES[5::-1]:
        acc = acc * v2 + coef
    cosine = acc * v
    twice = cosine + cosine
    out = [value, value * cosine]
    for _ in range(NRAD - 2):
        out.append(twice * out[-1] - out[-2])
    return [b.astype(BF16) for b in out]


def flipped(block):
    return block.astype(F32).T.astype(BF16)


def kernel(
    nx, ny,
    pos_hbm, feat_hbm, senders_hbm, counts_hbm, rad_hbm, mix_hbm, square_hbm, cot_hbm,
    updated_ref, grad_ref,
    pos, feat, senders, counts, rad, mix, square, cot,
    gpos, stack, basis, rows, gbasis, far_pos, far_feat, out_grad, in_grad,
    weight, own_col, cot_t, mix_t, square_t, grad_first, sums,
    local, psend, precv, fsend, frecv, gsend, grecv, far_precv, far_frecv, ready,
):
    gx = lax.axis_index("gx")
    gy = lax.axis_index("gy")
    half = ny // 2
    is_down = (gy == 0) | (gy == half)
    is_up = (gy == half - 1) | (gy == ny - 1)
    is_next = (gy == half - 2) | (gy == ny - 2)
    at_end = is_up & ((lax.rem(gx, 4) == 3) | (gx == 0))
    near = jnp.where(lax.rem(gx, 4) == 0, 2, 1)

    sign = jnp.where(is_up, -1, 1)

    def cell(dx, dy):
        return (lax.rem(gx + dx + nx, nx), lax.rem(gy + dy + ny, ny))

    def step_y(r):
        return jnp.where(r == 0, 0, jnp.where(r == 1, sign, -sign))

    def peer(r, q):
        return cell(DX[q], step_y(r))

    def mirrored(r, q):
        dy = step_y(r)
        there = lax.rem(gy + dy + ny, ny)
        sign_there = jnp.where((there == half - 1) | (there == ny - 1), -1, 1)
        return 3 * jnp.where(dy == 0, 0, jnp.where(dy == -sign_there, 1, 2)) + (3 - q) % 3

    loads = [
        pltpu.make_async_copy(src, dst, local.at[n])
        for n, src, dst in (
            (0, feat_hbm, feat), (1, pos_hbm, pos), (2, cot_hbm, cot), (2, mix_hbm, mix), (2, square_hbm, square),
            (3, rad_hbm, rad), (4, senders_hbm, senders), (5, counts_hbm, counts))
    ]
    barrier = pltpu.get_barrier_semaphore()

    def announce(device):
        pl.semaphore_signal(barrier, inc=1, device_id=device, device_id_type=MESH)

    for r, q in ((0, 1), (0, 2), (1, 0), (1, 1), (1, 2)):
        announce(peer(r, q))
    for q in range(3):
        @pl.when(jnp.logical_not(is_up))
        def _():
            announce(peer(2, q))

        @pl.when(is_down)
        def _():
            announce(cell(DX[q], half))

    @pl.when(is_down)
    def _():
        announce(cell(0, half - 1))

    for load in loads:
        load.start()
    loads[0].wait()
    own_feat = flipped(feat[0, 0])
    stack[0, 0:CH, :] = own_feat
    loads[1].wait()
    pl.semaphore_wait(barrier, 8 + jnp.where(is_up, 1, 0))

    @pl.when(is_up)
    def _():
        pl.semaphore_signal(ready, inc=1, device_id=cell(0, 1 - half), device_id_type=MESH)

    def halo_copy(kind, r, q):
        p, there = 3 * r + q, mirrored(r, q)
        if kind == 0:
            return pltpu.make_async_remote_copy(
                src_ref=pos.at[0, 0], dst_ref=gpos.at[there], send_sem=psend,
                recv_sem=precv.at[there], device_id=peer(r, q), device_id_type=MESH)
        return pltpu.make_async_remote_copy(
            src_ref=stack.at[0, pl.ds(0, CH)], dst_ref=stack.at[there, pl.ds(0, CH)], send_sem=fsend,
            recv_sem=frecv.at[there], device_id=peer(r, q), device_id_type=MESH)

    def far_copy(kind, q):
        there = (3 - q) % 3
        if kind == 0:
            return pltpu.make_async_remote_copy(
                src_ref=pos.at[0, 0], dst_ref=far_pos.at[there], send_sem=psend,
                recv_sem=far_precv, device_id=cell(DX[q], half), device_id_type=MESH)
        return pltpu.make_async_remote_copy(
            src_ref=stack.at[0, pl.ds(0, CH)], dst_ref=far_feat.at[there], send_sem=fsend,
            recv_sem=far_frecv, device_id=cell(DX[q], half), device_id_type=MESH)

    def relay_copy(kind, q):
        if kind == 0:
            return pltpu.make_async_remote_copy(
                src_ref=far_pos.at[q], dst_ref=gpos.at[6 + q], send_sem=psend,
                recv_sem=precv.at[6 + q], device_id=cell(0, half - 1), device_id_type=MESH)
        return pltpu.make_async_remote_copy(
            src_ref=far_feat.at[q], dst_ref=stack.at[6 + q, pl.ds(0, CH)], send_sem=fsend,
            recv_sem=frecv.at[6 + q], device_id=cell(0, half - 1), device_id_type=MESH)

    def sent(ref, sem):
        pltpu.make_async_remote_copy(
            src_ref=ref, dst_ref=ref, send_sem=sem, recv_sem=far_precv,
            device_id=peer(0, 1), device_id_type=MESH).wait_send()

    def arrived(ref, sem):
        pltpu.make_async_remote_copy(
            src_ref=ref, dst_ref=ref, send_sem=gsend, recv_sem=sem,
            device_id=peer(0, 1), device_id_type=MESH).wait_recv()

    def grad_copy(r, q):
        p, there = 3 * r + q, mirrored(r, q)
        return pltpu.make_async_remote_copy(
            src_ref=out_grad.at[p], dst_ref=in_grad.at[there], send_sem=gsend,
            recv_sem=grecv.at[there // 6], device_id=peer(r, q), device_id_type=MESH)

    def start(kind, directions):
        for r, q in directions:
            halo_copy(kind, r, q).start()

    @pl.when(is_up)
    def _():
        for direction in ((2, 1), (2, 2), (2, 0), (0, 1), (0, 2), (1, 0)):
            for kind in range(2):
                start(kind, (direction,))

    for kind in range(2):
        @pl.when(is_down)
        def _():
            for q in (1, 2, 0):
                far_copy(kind, q).start()

        @pl.when(jnp.logical_not(is_up))
        def _():
            start(kind, ((1, 1), (1, 2), (1, 0)))

        @pl.when(jnp.logical_not(is_up | is_next))
        def _():
            start(kind, ((0, 1), (0, 2)))

        @pl.when(jnp.logical_not(is_up | is_next | is_down))
        def _():
            start(kind, ((2, 1), (2, 2), (2, 0)))

    own_rows = pos[0, 0].astype(F32)
    own_x = [own_rows[m:m + 1, :] for m in range(3)]
    columns = jnp.concatenate([own_rows, jnp.zeros((BLK - 3, BLK), F32)], axis=0).T
    for m in range(3):
        own_col[m] = jnp.broadcast_to(columns[:, m:m + 1], (BLK, BLK))
    pltpu.make_async_copy(far_feat, far_feat, local.at[2]).wait()
    for load in loads[5:]:
        load.wait()
    count = counts[0, 0, 0]
    radial_rows = jnp.concatenate([rad[0], rad[1], jnp.zeros((BLK - 2 * NRAD, CH), F32)], axis=0).T
    for n in range(2 * NRAD):
        weight[n] = jnp.broadcast_to(radial_rows[:, n:n + 1], (CH, BLK))
    cot_t[...] = flipped(cot[0, 0])
    mix_t[...] = flipped(mix[...])
    square_t[...] = flipped(square[...])
    grad_first[...] = jnp.dot(mix[...], cot_t[...], preferred_element_type=F32)
    diagonal = lax.broadcasted_iota(jnp.int32, (BLK, BLK), 0) == lax.broadcasted_iota(jnp.int32, (BLK, BLK), 1)

    def tile_basis(p, own):
        dx = lax.rem(2 * lax.rem(p, 3) + 1, 3) - 1
        dy = step_y(lax.div(p, 3))
        g = 3 * (dx + 1) + dy + 1
        live = jnp.int32(0)
        for t in range(8):
            live = live + jnp.where((senders[0, 0, 0, t] == g) & (t < count), 1, 0)
        keep = jnp.full((BLK, BLK), live.astype(F32))
        if own:
            keep = jnp.where(diagonal, 0.0, keep)
        axis_of = lax.broadcasted_iota(jnp.int32, (3, BLK), 0)
        shift = jnp.where(axis_of == 0, dx.astype(F32), jnp.where(axis_of == 1, dy.astype(F32), 0.0))
        place = (pos[0, 0] if own else gpos[p]).astype(F32) + shift
        for m in range(3):
            rows[p, m:m + 1, :] = place[m:m + 1, :]
        offsets = [place[m:m + 1, :] - own_col[m] for m in range(3)]
        for k, b in enumerate(radial(*offsets, keep)):
            basis[p, k * BLK:(k + 1) * BLK, :] = b

    def tile_stack(p):
        h = stack[p, 0:CH, :].astype(F32)
        for m in range(3):
            stack[p, (m + 1) * CH:(m + 2) * CH, :] = (rows[p, m:m + 1, :] * h).astype(BF16)

    def gather(blocks, begin=False):
        left = jnp.concatenate([stack[p] for p in blocks], axis=1)
        for pair in range(NRAD // 2):
            span = slice(2 * pair * BLK, 2 * (pair + 1) * BLK)
            right = jnp.concatenate([basis[p, span, :] for p in blocks], axis=1)
            product = lax.dot_general(left, right, NT, preferred_element_type=F32)
            for n in range(5):
                block = max(n - 1, 0)
                part = product[block * CH:(block + 1) * CH]
                w = 0 if n == 0 else NRAD
                term = weight[w + 2 * pair] * part[:, :BLK] + weight[w + 2 * pair + 1] * part[:, BLK:]
                if begin and pair == 0:
                    sums[n] = term
                else:
                    sums[n] += term

    tile_basis(jnp.int32(0), True)
    tile_stack(0)

    def place(first, stop, number):
        @pl.loop(first, stop)
        def _(n):
            p = number(n)
            arrived(gpos.at[p], precv.at[p])
            tile_basis(p, False)

    def collect(first, stop, number):
        @pl.loop(first, stop)
        def _(n):
            p = number(n)
            arrived(stack.at[p, pl.ds(0, CH)], frecv.at[p])
            tile_stack(p)

    def receive(count, number):
        place(0, count, number)
        collect(0, count, number)

    receive(1, lambda n: n + 3)
    gather((0, 3), begin=True)

    for kind in range(2):
        @pl.when(is_up)
        def _():
            start(kind, ((1, 1), (1, 2)))

        @pl.when(is_next)
        def _():
            start(kind, ((0, 1), (0, 2), (2, 1), (2, 2), (2, 0)))

    later = 3 - near
    receive(2, lambda n: near + 3 * n)
    gather((near, near + 3))
    receive(2, lambda n: jnp.where(at_end, 6 + n, later + 3 * n))

    @pl.when(is_down)
    def _():
        arrived(far_pos, far_precv)
        arrived(far_feat, far_frecv)
        pl.semaphore_wait(ready, 1)
        for kind in range(2):
            for q in range(3):
                relay_copy(kind, q).start()

    early = jnp.where(is_down & (gx == nx - 1), 8, jnp.where(is_down & (gx == 0), 7, 6))
    middle = jnp.where(at_end, 8, early)
    last = (
        jnp.where(at_end, later, jnp.where(early == 6, 7, 6)),
        jnp.where(at_end, later + 3, jnp.where(early == 8, 7, 8)),
    )

    def order(n):
        return jnp.where(n == 0, middle, jnp.where(n == 1, last[0], last[1]))

    ahead = jnp.where(at_end, 1, 3)
    place(0, ahead, order)
    collect(0, 1, order)
    gather((jnp.where(at_end, 6, later), jnp.where(at_end, 7, later + 3), middle))
    place(ahead, 3, order)
    collect(1, 3, order)
    gather(last)

    sum_one = sums[1]
    second = [(sums[2 + m] - own_x[m] * sum_one).astype(BF16) for m in range(3)]
    quadratic = jnp.dot(square_t[...], jnp.concatenate(second, axis=1), preferred_element_type=F32)
    quad = [quadratic[:, m * BLK:(m + 1) * BLK] for m in range(3)]
    second_f = [s.astype(F32) for s in second]
    cot_f = cot_t[...].astype(F32)
    weighted = jnp.concatenate([(cot_f * s).astype(BF16) for s in second_f], axis=1)
    through = jnp.dot(square[...], weighted, preferred_element_type=F32)
    grad_second = [cot_f * quad[m] + through[:, m * BLK:(m + 1) * BLK] for m in range(3)]
    grad_one = -(own_x[0] * grad_second[0] + own_x[1] * grad_second[1] + own_x[2] * grad_second[2])
    for k in range(NRAD):
        lanes = slice(k * BLK, (k + 1) * BLK)
        w0, w1 = weight[k], weight[NRAD + k]
        gbasis[0:CH, lanes] = (w0 * grad_first[...] + w1 * grad_one).astype(BF16)
        for m in range(3):
            gbasis[(m + 1) * CH:(m + 2) * CH, lanes] = (w1 * grad_second[m]).astype(BF16)

    def pull(blocks):
        right = jnp.concatenate([basis[p] for p in blocks], axis=1)
        halves = [
            jnp.dot(gbasis[2 * n * CH:2 * (n + 1) * CH, :], right, preferred_element_type=F32)
            for n in range(2)
        ]
        out = []
        for n, p in enumerate(blocks):
            lanes = slice(n * BLK, (n + 1) * BLK)
            part = [halves[m // 2][m % 2 * CH:(m % 2 + 1) * CH, lanes] for m in range(4)]
            total = part[0]
            for m in range(3):
                total = total + rows[p, m:m + 1, :] * part[m + 1]
            out.append(total)
        return out

    first = jnp.where(is_up, 2, 1)
    second_row = 3 - first
    for blocks in (
        ((first, 1), (first, 2)), ((first, 0), (0, 1)), ((second_row, 1), (second_row, 2)), ((second_row, 0), (0, 2))):
        totals = pull([3 * row + q for row, q in blocks])
        for (row, q), total in zip(blocks, totals):
            out_grad[3 * row + q] = total.astype(BF16)
        for row, q in blocks:
            grad_copy(row, q).start()

    linear = jnp.dot(mix_t[...], sums[0].astype(BF16), preferred_element_type=F32)
    square_sum = quad[0] * second_f[0] + quad[1] * second_f[1] + quad[2] * second_f[2]
    updated_ref[0] = linear.T
    updated_ref[1] = square_sum.T
    grad_ref[0] = pull((0,))[0].T
    total = None
    for first, last in ((1, 6), (6, 9)):
        arrived(in_grad.at[pl.ds(first, last - first)], grecv.at[first // 6])
        for p in range(first, last):
            came = in_grad[p].astype(F32)
            total = came if total is None else total + came
    grad_ref[1] = total.T
    sent(gpos.at[pl.ds(1, 8)], psend)
    sent(in_grad.at[pl.ds(1, 8)], fsend)
    sent(in_grad.at[pl.ds(1, 8)], gsend)

    @pl.when(is_down)
    def _():
        sent(far_pos, psend)
        sent(far_feat, fsend)


def solution(mesh):
    nx, ny = mesh.shape["gx"], mesh.shape["gy"]

    def body(positions, features, senders, counts, radial_w, mix_w, square_w, cotangent):
        hbm = pl.BlockSpec(memory_space=pltpu.HBM)
        dma = pltpu.SemaphoreType.DMA
        vmem = pl.BlockSpec(memory_space=pltpu.VMEM)
        parts = pl.pallas_call(
            functools.partial(kernel, nx, ny),
            out_shape=(pltpu.VMEM((2, BLK, CH), F32), pltpu.VMEM((2, BLK, CH), F32)),
            in_specs=[hbm] * 8,
            out_specs=(vmem, vmem),
            scratch_shapes=[
                pltpu.VMEM(positions.shape, BF16),
                pltpu.VMEM(features.shape, BF16),
                pltpu.SMEM(senders.shape, jnp.int32),
                pltpu.SMEM(counts.shape, jnp.int32),
                pltpu.VMEM(radial_w.shape, F32),
                pltpu.VMEM(mix_w.shape, BF16),
                pltpu.VMEM(square_w.shape, BF16),
                pltpu.VMEM(cotangent.shape, BF16),
                pltpu.VMEM((GHOSTS, 3, BLK), BF16),
                pltpu.VMEM((GHOSTS, 4 * CH, BLK), BF16),
                pltpu.VMEM((GHOSTS, NRAD * BLK, BLK), BF16),
                pltpu.VMEM((GHOSTS, 8, BLK), F32),
                pltpu.VMEM((4 * CH, NRAD * BLK), BF16),
                pltpu.VMEM((3, 3, BLK), BF16),
                pltpu.VMEM((3, CH, BLK), BF16),
                pltpu.VMEM((GHOSTS, CH, BLK), BF16),
                pltpu.VMEM((GHOSTS, CH, BLK), BF16),
                pltpu.VMEM((2 * NRAD, CH, BLK), F32),
                pltpu.VMEM((3, BLK, BLK), F32),
                pltpu.VMEM((CH, BLK), BF16),
                pltpu.VMEM((CH, CH), BF16),
                pltpu.VMEM((CH, CH), BF16),
                pltpu.VMEM((CH, BLK), F32),
                pltpu.VMEM((5, CH, BLK), F32),
                dma((6,)),
                dma, dma((GHOSTS,)), dma, dma((GHOSTS,)), dma, dma((2,)),
                dma, dma,
                pltpu.SemaphoreType.REGULAR,
            ],
            compiler_params=pltpu.CompilerParams(collective_id=0, has_side_effects=True),
            name="layer",
        )(positions, features, senders, counts, radial_w, mix_w, square_w, cotangent)
        updated, grad = lax.reduce(
            parts, (jnp.float32(0), jnp.float32(0)), lambda a, b: (a[0] + b[0], a[1] + b[1]), (0,))
        return updated.astype(BF16)[None, None], grad[None, None]

    placed = (
        P("gx", "gy", None, None),
        P("gx", "gy", None, None),
        P("gx", "gy", None, None),
        P("gx", "gy", None),
        P(),
        P(),
        P(),
        P("gx", "gy", None, None),
    )
    return jax.shard_map(
        body,
        mesh=mesh,
        in_specs=placed,
        out_specs=(P("gx", "gy", None, None), P("gx", "gy", None, None)),
        check_vma=False,
    )
```
